32 devices in a mesh: by: 4 (over y, x), bz: 8 (over z, core).
Axes of the slice: x: 2, y: 2, z: 4, core: 2. Of those that a mesh axis runs over, the one named last changes fastest.
Arguments:
- camera_tiles: bfloat16 [128, 2, 256, 4, 128], P('bz', None, 'by'), may hold values from 0.05 to 5
- tile_block: int32 [128, 1], replicated, may hold values from 0 to 7; in each aligned block of 16 rows (0 to 15, 16 to 31, ...) at most 4 rows name the same one
- tile_offset: int32 [128], replicated, may hold values from 0 to 63
- band_index: int32 [256], P('by'), may hold values from 0 to 8
- interp: bfloat16 [256, 2], P('by'), may hold values from 0.19921875 to 1
- psf_taps: float32 [2, 3, 31], replicated, may hold values from 0.02 to 1
- background: float32 [2], replicated, may hold values from 0.05 to 0.5
Outputs:
- deskewed: float32 [2, 256, 512, 128], P(None, 'by', 'bz')
- estimate: float32 [2, 256, 512, 128], P(None, 'by', 'bz')
The draws below stay inside these ranges and needn't reach their ends.
Inputs may be any that keep to these rules, and one draw needn't show every extreme that they name: `tile_block`: within the tiles of one device along bz (aligned blocks of 16 rows) no block index is named by more than 4 tiles, and in some such block one index is named by exactly 4.
All inputs are finite; a program needn't handle non-finite values.
Results may differ from the reference program's by a relative error of at most 0.0006.
Values may be sent and summed in bfloat16 or wider, within the bound.
No kernel may reach another device: no remote copies, remote signals or barrier semaphores. Data moves between devices by JAX's collectives and lax.ppermute only.
A program may use at most 128 MiB of HBM per device.

```python
import math
import jax
import jax.numpy as jnp
import numpy as np
from jax import lax

C = 2
TAPS = 31
SHIFT = 8
PLANES = 4
ITERS = 2
Z_DEV = 64
XLEN = 128
TILES_DEV = 16
CAP = 4
TILES = 128
NY = 256
NZ = 512
N_BZ = 8


def draw_camera_tiles(key, part):
    shape = (TILES, C, NY, PLANES, XLEN)
    first_key = jax.random.fold_in(key, 11)
    level = jax.random.uniform(first_key, shape, jnp.float32)
    values = 0.05 * jnp.power(100.0, level)
    return values.astype(jnp.float32).astype(jnp.bfloat16)


def touch_ends(values, rng, least, high):
    place = [jax.random.randint(jax.random.fold_in(rng, axis), (), 0, length) for axis, length in enumerate(values.shape)]
    widest = values.shape.index(max(values.shape))
    beside = place[:widest] + [(place[widest] + 1) % values.shape[widest]] + place[widest + 1:]
    return values.at[tuple(place)].set(least).at[tuple(beside)].set(high)


def block_scale(own_key, dims, pieces, least, largest):
    def one(dim, parts):
        draws = jax.random.uniform(jax.random.fold_in(jax.random.fold_in(own_key, 6), dim), (parts,), jnp.float32, least / len(pieces), largest / len(pieces))
        return jnp.repeat(jnp.exp(draws), dims[dim] // parts).reshape((-1,) + (1,) * (len(dims) - dim - 1))

    gain = one(*pieces[0])
    for cut in pieces[1:]:
        gain = gain * one(*cut)
    return gain


def routed_block(rng, own, number, rows, number_of, top, most, skew):
    order = jax.random.permutation(rng, number_of)
    crowded, usual = portions_of(number_of, rows * top, most, skew, True), portions_of(number_of, rows * top, most, skew, False)
    places = jnp.arange(number_of)

    def named(tallies, rotation):
        used = int((tallies > 0).sum())
        fixed = max(1, used // 4)
        passed = fixed + (places - fixed + rotation * (used - fixed)) % max(1, number_of - fixed)
        return jnp.zeros((number_of,), jnp.int32).at[order[jnp.where(places < fixed, places, passed)]].set(jnp.asarray(tallies, jnp.int32))

    tallies = jnp.where(number % 4 == 0, named(crowded, number // 4), named(usual, number - number // 4 - 1))
    mixed = jax.random.permutation(jax.random.fold_in(own, 3), number_of)
    donor, sink = mixed[0:number_of // 2 * 2:2], mixed[1:number_of // 2 * 2:2]
    margin = jnp.minimum(tallies[donor] - 1, most - tallies[sink]) // 2
    margin = jnp.where((donor == order[0]) | (sink == order[0]) | (tallies[sink] == 0), 0, jnp.maximum(margin, 0))
    passed = jax.random.randint(jax.random.fold_in(own, 4), (number_of // 2,), 0, 1 << 20) % (margin + 1)
    tallies = tallies.at[donor].add(-passed).at[sink].add(passed)
    labels = jnp.searchsorted(jnp.cumsum(tallies), jnp.arange(rows * top), side="right").astype(jnp.int32)
    grid = labels.reshape(top, rows).T
    grid = grid[jax.random.permutation(jax.random.fold_in(own, 1), rows)]
    rotation = jax.random.randint(jax.random.fold_in(own, 2), (rows, 1), 0, top)
    return jnp.take_along_axis(grid, (jnp.arange(top)[None, :] + rotation) % top, axis=1)


def portions_of(count, total, reach, slope, full):
    portions = [(1 << 20) // math.isqrt(rank ** slope) + 1 for rank in range(1, count + 1)]
    largest = reach if full else min(reach, max(-(-total // count), total * portions[0] // sum(portions)))
    least = 1 if total - largest >= count - 1 else 0
    counts, spare = [largest] + [least] * (count - 1), total - largest - least * (count - 1)
    while spare > 0:
        movable = [i for i in range(1, count) if counts[i] < largest] or [i for i in range(1, count) if counts[i] < reach]
        mass, remaining = sum([portions[i] for i in movable]), spare
        for i in movable:
            extra = min(reach - counts[i], max(1, remaining * portions[i] // mass), spare)
            counts[i] = counts[i] + extra
            spare = spare - extra
    return np.array(counts)


def setup_inputs(seed: int = 0) -> dict:
    seeds = jax.random.split(jax.random.key(seed), 8)
    camera_tiles = draw_camera_tiles(jax.random.fold_in(seeds[7], 71), 0)
    tile_block_keys = jax.random.split(jax.random.fold_in(seeds[1], 1), TILES // TILES_DEV)
    tile_block_turns = jax.random.permutation(jax.random.fold_in(seeds[1], 3), TILES // TILES_DEV)
    tile_block = jax.vmap(lambda own, number: routed_block(jax.random.fold_in(seeds[1], 2), own, number, TILES_DEV, N_BZ, 1, CAP, 2))(tile_block_keys, tile_block_turns).reshape((TILES, 1))
    tile_offset = touch_ends(jax.random.randint(seeds[2], (TILES,), 0, Z_DEV), jax.random.fold_in(seeds[2], 1), 0, Z_DEV - 1).astype(jnp.int32)
    band_index = touch_ends(jax.random.randint(seeds[3], (NY,), 0, SHIFT + 1), jax.random.fold_in(seeds[3], 1), 0, SHIFT).astype(jnp.int32)
    interp = jnp.clip(0.19921875 + 0.80078125 * jax.random.uniform(seeds[4], (NY, 2), jnp.float32) ** block_scale(seeds[4], (NY, 2), ((0, 4),), -0.2, 0.2), 0.19921875, 1.0).astype(jnp.bfloat16)
    psf_taps = jnp.clip(jnp.exp(jax.random.uniform(seeds[5], (C, 3, TAPS), jnp.float32, math.log(0.02), math.log(1.0))), 0.02, 1.0)
    background = jnp.clip(jnp.exp(jax.random.uniform(seeds[6], (C,), jnp.float32, math.log(0.05), math.log(0.5))), 0.05, 0.5)
    return {"camera_tiles": camera_tiles, "tile_block": tile_block, "tile_offset": tile_offset, "band_index": band_index, "interp": interp, "psf_taps": psf_taps, "background": background}


def correlate_axis(volume, tap_rows, direction):
    reach_cells = tap_rows.shape[1] // 2
    widths = [(0, 0), (0, 0), (0, 0), (0, 0)]
    widths[direction] = (reach_cells, reach_cells)
    padded = jnp.pad(volume, widths)
    length = volume.shape[direction]
    running = jnp.zeros(volume.shape, jnp.float32)
    for shift_tap in range(tap_rows.shape[1]):
        running = running + tap_rows[:, shift_tap][:, None, None, None] * lax.slice_in_dim(padded, shift_tap, shift_tap + length, axis=direction)
    return running


def blur_volume(volume, kernels):
    along_y = correlate_axis(volume, kernels[:, 0], 1)
    along_z = correlate_axis(along_y, kernels[:, 1], 2)
    return correlate_axis(along_z, kernels[:, 2], 3)


def reference(camera_tiles, tile_block, tile_offset, band_index, interp, psf_taps, background):
    tile_count, channels, height, planes, line_len = camera_tiles.shape
    span_len = planes + SHIFT + 1
    position = jnp.arange(span_len, dtype=jnp.int32)[None, :, None]
    first_cell = band_index.astype(jnp.int32)[:, None, None] + jnp.arange(planes, dtype=jnp.int32)[None, None, :]
    near_weight = interp[:, 0].astype(jnp.float32)[:, None, None]
    far_weight = interp[:, 1].astype(jnp.float32)[:, None, None]
    weights = jnp.where(position == first_cell, near_weight, 0.0) + jnp.where(position == first_cell + 1, far_weight, 0.0)
    canvas = jnp.zeros((channels, height, NZ + span_len, line_len), jnp.float32)

    def add_tile(canvas, tile_entry):
        raw_tile, block_index, offset_cell = tile_entry
        contribution = jnp.einsum('yls,cysx->cylx', weights, raw_tile.astype(jnp.float32), precision=lax.Precision.HIGHEST)
        start_cell = (block_index * Z_DEV + offset_cell).astype(jnp.int32)
        current = lax.dynamic_slice_in_dim(canvas, start_cell, span_len, 2)
        return lax.dynamic_update_slice_in_dim(canvas, current + contribution, start_cell, 2), None

    canvas, _ = lax.scan(add_tile, canvas, (camera_tiles, tile_block[:, 0], tile_offset))
    deskewed = canvas[:, :, :NZ]
    kernels = psf_taps / jnp.sum(psf_taps, axis=2, keepdims=True)
    flipped = kernels[:, :, ::-1]
    backdrop = background[:, None, None, None]
    estimate = deskewed + backdrop
    for iteration in range(ITERS):
        blurred = blur_volume(estimate, kernels)
        quotient = deskewed / (blurred + backdrop)
        estimate = estimate * blur_volume(quotient, flipped)
    return deskewed, estimate
```

```python
import functools

import jax
import jax.numpy as jnp
from jax import lax
from jax.experimental import pallas as pl
from jax.experimental.pallas import tpu as pltpu
from jax.sharding import PartitionSpec as P


SHIFT = 8
ITERS = 2
Z_DEV = 64
HALO = 16
F32 = jnp.float32
BF16 = jnp.bfloat16


def in_vmem(count):
    return [pl.BlockSpec(memory_space=pltpu.VMEM) for _ in range(count)]


def place_kernel(channel_ref, own_ref, other_ref, out_ref, sems):
    rows = other_ref.shape[0]
    channel = channel_ref[0]
    copies = [
        pltpu.make_async_copy(own_ref.at[pl.ds(channel * rows, rows)], out_ref.at[channel], sems.at[0]),
        pltpu.make_async_copy(other_ref, out_ref.at[1 - channel], sems.at[1]),
    ]
    for copy in copies:
        copy.start()
    for copy in copies:
        copy.wait()


def place_halves(channel, both_rows, other):
    return pl.pallas_call(
        place_kernel,
        out_shape=jax.ShapeDtypeStruct((2,) + other.shape, other.dtype),
        in_specs=[pl.BlockSpec(memory_space=pltpu.SMEM)] + in_vmem(2),
        out_specs=pl.BlockSpec(memory_space=pl.ANY),
        scratch_shapes=[pltpu.SemaphoreType.DMA((2,))],
        compiler_params=pltpu.CompilerParams(vmem_limit_bytes=40 << 20),
        name="place_halves",
    )(channel[None], both_rows, other)


def gather_planes_kernel(starts_ref, arrived_ref, planes_ref, over_ref):
    halves, slots, planes, rows = arrived_ref.shape[:4]
    reach = over_ref.shape[0]
    height = planes_ref.shape[0]

    def clear(z, carry):
        planes_ref[z] = jnp.zeros(planes_ref.shape[1:], F32)
        return carry

    lax.fori_loop(0, height, clear, 0)

    def add(j, carry):
        start = starts_ref[j]

        @pl.when(start >= 0)
        def _():
            for s in range(planes):
                for h in range(halves):
                    here = pl.ds(h * rows, rows)
                    planes_ref[start + s, here, :] += arrived_ref[h, j, s].astype(F32)

        return carry

    lax.fori_loop(0, slots, add, 0)
    over_ref[...] = planes_ref[height - reach:]


def gather_planes(arrived, starts):
    halves, _, planes, rows, nx = arrived.shape
    height = Z_DEV + planes - 1
    return pl.pallas_call(
        gather_planes_kernel,
        out_shape=[
            jax.ShapeDtypeStruct((height, halves * rows, nx), F32),
            jax.ShapeDtypeStruct((SHIFT + planes, halves * rows, nx), F32),
        ],
        in_specs=[pl.BlockSpec(memory_space=pltpu.SMEM)] + in_vmem(1),
        out_specs=in_vmem(2),
        compiler_params=pltpu.CompilerParams(vmem_limit_bytes=40 << 20),
        name="gather_planes",
    )(starts, arrived)


def deskew_kernel(backdrop_ref, band_ref, near_ref, far_ref, planes_ref, before_ref,
                  out_ref, cast_ref, out_low_ref, out_high_ref, all_ref, *, pitch):
    ny, nz = out_ref.shape[:2]
    reach = before_ref.shape[0]
    ahead = SHIFT + 1
    backdrop = backdrop_ref[0]
    for z in range(ahead + nz):
        if z < ahead:
            plane = before_ref[z]
        elif z < reach:
            plane = before_ref[z] + planes_ref[z - ahead]
        else:
            plane = planes_ref[z - ahead]
        all_ref[pl.ds(z * pitch, ny), :] = plane

    def row(y, carry):
        first = (ahead - band_ref[y]) * pitch + y
        value = near_ref[y] * all_ref[pl.ds(first, nz, stride=pitch), :]
        value = value + far_ref[y] * all_ref[pl.ds(first - pitch, nz, stride=pitch), :]
        out_ref[y] = value
        cast = (value + backdrop).astype(BF16)
        cast_ref[y] = cast
        out_low_ref[y] = cast[:HALO]
        out_high_ref[y] = cast[nz - HALO:]
        return carry

    lax.fori_loop(0, ny, row, 0, unroll=4)


def deskew(backdrop, band, near, far, planes, before):
    ny, nx = planes.shape[1:]
    pitch = ny + 8
    smem = [pl.BlockSpec(memory_space=pltpu.SMEM)] * 4
    return pl.pallas_call(
        functools.partial(deskew_kernel, pitch=pitch),
        out_shape=[
            jax.ShapeDtypeStruct((ny, Z_DEV, nx), F32),
            jax.ShapeDtypeStruct((ny, Z_DEV, nx), BF16),
            jax.ShapeDtypeStruct((ny, HALO, nx), BF16),
            jax.ShapeDtypeStruct((ny, HALO, nx), BF16),
        ],
        in_specs=smem + in_vmem(2),
        out_specs=in_vmem(4),
        scratch_shapes=[pltpu.VMEM(((Z_DEV + SHIFT + 1) * pitch, nx), F32)],
        compiler_params=pltpu.CompilerParams(vmem_limit_bytes=40 << 20),
        name="deskew",
    )(backdrop, band, near, far, planes, before)


def blur_kernel(backdrop_ref, own_ref, low_ref, high_ref, side_ref, side_low_ref, side_high_ref,
                mx_ref, mz_ref, my_ref, point_ref, *rest, quotient, first, ny, nz, nside):
    if quotient:
        cast_ref, out_low_ref, out_high_ref, mid_ref, blur_ref = rest
    else:
        full_ref, cast_ref, out_low_ref, out_high_ref, mid_ref, blur_ref = rest
    total = ny + nside
    mx, mz, my = mx_ref[...], mz_ref[...], my_ref[...]
    lanes = mx.shape[1]
    pitch = nz + 8
    width = nz + 2 * HALO
    group = 16
    ahead = 8

    def planes(load, base, count):
        def body(g, carry):
            pieces = []
            for k in range(group):
                pieces += list(load(g * group + k))
            stack = jnp.concatenate(pieces, axis=0)
            alongx = jnp.dot(jnp.concatenate([stack, stack], axis=1), mx, preferred_element_type=F32)
            alongx = alongx.astype(BF16)
            for k in range(0, group, 2):
                pair = jnp.concatenate(
                    [alongx[k * width:(k + 1) * width], alongx[(k + 1) * width:(k + 2) * width]], axis=1
                )
                both = jnp.dot(mz, jnp.concatenate([pair, pair], axis=0), preferred_element_type=F32)
                row = pl.multiple_of((base + g * group + k) * pitch, 8)
                mid_ref[pl.ds(row, nz), :] = both[:, :lanes]
                mid_ref[pl.ds(row + pitch, nz), :] = both[:, lanes:]
            return carry

        lax.fori_loop(0, count // group, body, 0)

    planes(lambda y: (low_ref[y], own_ref[y], high_ref[y]), 0, ny)
    planes(lambda y: (side_low_ref[y], side_ref[y], side_high_ref[y]), ny, nside)

    def split(z):
        column = mid_ref[pl.ds(z, total, stride=pitch), :]
        head = column.astype(BF16)
        tail = (column - head.astype(F32)).astype(BF16)
        return jnp.concatenate([head, tail, head], axis=0)

    def columns(g, carry):
        for k in range(ahead):
            z = (g * ahead + k) * 2
            both = jnp.dot(my, jnp.concatenate([split(z), split(z + 1)], axis=1), preferred_element_type=F32)
            blur_ref[pl.ds(z, ny, stride=pitch), :] = both[:, :lanes]
            blur_ref[pl.ds(z + 1, ny, stride=pitch), :] = both[:, lanes:]
        return carry

    lax.fori_loop(0, nz // (2 * ahead), columns, 0)
    backdrop = backdrop_ref[0]

    def finish(y, carry):
        row = pl.multiple_of(y * pitch, 8)
        blurred = blur_ref[pl.ds(row, nz), :]
        if quotient:
            value = point_ref[y] / (blurred + backdrop)
        else:
            value = (point_ref[y] + backdrop if first else point_ref[y]) * blurred
            full_ref[y] = value
        cast = value.astype(BF16)
        cast_ref[y] = cast
        out_low_ref[y] = cast[:HALO]
        out_high_ref[y] = cast[nz - HALO:]
        return carry

    lax.fori_loop(0, ny, finish, 0, unroll=8)


def blur_block(quotient, first, backdrop, field, halos, matrices, point):
    ny, nz, nx = field[0].shape
    nside = halos[2].shape[0]
    outs = [
        jax.ShapeDtypeStruct((ny, nz, nx), BF16),
        jax.ShapeDtypeStruct((ny, HALO, nx), BF16),
        jax.ShapeDtypeStruct((ny, HALO, nx), BF16),
    ]
    if not quotient:
        outs = [jax.ShapeDtypeStruct((ny, nz, nx), F32)] + outs
    return pl.pallas_call(
        functools.partial(blur_kernel, quotient=quotient, first=first, ny=ny, nz=nz, nside=nside),
        out_shape=outs,
        in_specs=[pl.BlockSpec(memory_space=pltpu.SMEM)] + in_vmem(10),
        out_specs=in_vmem(len(outs)),
        scratch_shapes=[
            pltpu.VMEM(((ny + nside) * (nz + 8), nx), F32),
            pltpu.VMEM((ny * (nz + 8), nx), F32),
        ],
        compiler_params=pltpu.CompilerParams(vmem_limit_bytes=56 << 20),
        cost_estimate=pl.CostEstimate(flops=20_000_000_000, transcendentals=0, bytes_accessed=16_000_000),
        name="blur_quotient" if quotient else "blur_estimate",
    )(backdrop, field[0], halos[0], halos[1], halos[2], halos[3], halos[4], *matrices, point)


def halo_exchange(field):
    block, face_low, face_high = field
    rows = block.shape[0]
    blocks = lax.axis_size("bz")
    wide = lax.axis_size("by")
    halves = wide // 2
    up = [(i, i + 1) for i in range(blocks - 1)]
    down = [(i + 1, i) for i in range(blocks - 1)]
    place = lax.axis_index("by") // 2

    if halves == 2:
        sides = [(jnp.where(place == 0, rows - HALO, 0), [(i, i ^ 2) for i in range(wide)])]
    else:
        sides = [
            (rows - HALO, [(i, i + 2) for i in range(wide - 2)]),
            (0, [(i + 2, i) for i in range(wide - 2)]),
        ]

    def both(pairs, step):
        return [
            (a * blocks + z, b * blocks + z + step)
            for a, b in pairs
            for z in range(blocks)
            if 0 <= z + step < blocks
        ]

    side, side_low, side_high = [], [], []
    for start, pairs in sides:
        cut = lambda x: lax.dynamic_slice_in_dim(x, start, HALO, 0)
        side.append(lax.ppermute(cut(block), "by", pairs))
        side_low.append(lax.ppermute(cut(face_high), ("by", "bz"), both(pairs, 1)))
        side_high.append(lax.ppermute(cut(face_low), ("by", "bz"), both(pairs, -1)))
    low = lax.ppermute(face_high, "bz", up)
    high = lax.ppermute(face_low, "bz", down)
    join = lambda parts: parts[0] if len(parts) == 1 else jnp.concatenate(parts, axis=0)
    return low, high, join(side), join(side_low), join(side_high)


def head_tail(matrix):
    head = lax.reduce_precision(matrix, 8, 7)
    return head.astype(BF16), (matrix - head).astype(BF16)


def band(taps, out_place, in_place):
    count = taps.shape[0]
    offset = in_place[None, :] - out_place[:, None] + count // 2
    matches = (offset[:, :, None] == jnp.arange(count)[None, None, :]).astype(F32)
    return jnp.einsum("ijw,cw->cij", matches, jnp.stack([taps, taps[::-1]]), precision=lax.Precision.HIGHEST)


def band_matrices(taps, ny, nz, nx):
    halves = lax.axis_size("by") // 2
    place = lax.axis_index("by") // 2
    before, after = jnp.arange(HALO) - HALO, jnp.arange(HALO) + ny
    if halves == 2:
        sides = [jnp.where(place == 0, after, before)]
    else:
        sides = [before, after]
    along = jnp.arange(nx)
    xh, xl = head_tail(band(taps[2], along, along)[::-1])
    zh, zl = head_tail(band(taps[1], jnp.arange(nz), jnp.arange(nz + 2 * HALO) - HALO))
    yh, yl = head_tail(band(taps[0], jnp.arange(ny), jnp.concatenate([jnp.arange(ny)] + sides)))
    mx = jnp.concatenate([xh, xl], axis=1)
    mz = jnp.concatenate([zh, zl], axis=2)
    my = jnp.concatenate([yh, yh, yl], axis=2)
    return (mx[0], mz[0], my[0]), (mx[1], mz[1], my[1])


def swap_pair(x):
    return lax.ppermute(x, "by", [(i, i ^ 1) for i in range(lax.axis_size("by"))])


def route_tiles(camera_tiles, tile_block, tile_offset):
    tile_count, channels = camera_tiles.shape[:2]
    blocks = lax.axis_size("bz")
    wide = lax.axis_size("by")
    capacity = max(2, 2 * tile_count // blocks)
    own_index = lax.axis_index("bz")
    targets = tile_block[:, 0].reshape(blocks, tile_count)
    offsets = tile_offset.reshape(blocks, tile_count)
    matches = (targets[:, :, None] == jnp.arange(blocks)[None, None, :]).astype(jnp.int32)
    places = jnp.sum((jnp.cumsum(matches, axis=1) - matches) * matches, axis=2)
    own_slot = lax.dynamic_index_in_dim(targets * capacity + places, own_index, 0, keepdims=False)
    slots = jnp.arange(blocks * capacity)
    tile_of = jnp.sum(
        jnp.where(own_slot[None, :] == slots[:, None], jnp.arange(tile_count)[None, :], 0), axis=1
    )
    rows = jnp.concatenate([tile_of * channels + c for c in range(channels)])
    planar = jnp.swapaxes(camera_tiles, 2, 3)
    outgoing = jnp.take(planar.reshape((tile_count * channels,) + planar.shape[2:]), rows, axis=0, mode="clip")
    outgoing = outgoing.reshape((channels * blocks, capacity) + planar.shape[2:])
    groups = [
        [(2 * j + c) * blocks + z for c in range(2) for z in range(blocks)] for j in range(wide // 2)
    ]
    arrived = lax.all_to_all(
        outgoing, ("by", "bz"), split_axis=0, concat_axis=0, axis_index_groups=groups, tiled=True
    )
    chosen = (targets[:, :, None] == own_index) & (
        places[:, :, None] == jnp.arange(capacity)[None, None, :]
    )
    starts = jnp.sum(jnp.where(chosen, offsets[:, :, None] + 1, 0), axis=1) - 1
    return (
        arrived.reshape((channels, blocks * capacity) + planar.shape[2:]),
        starts.reshape(blocks * capacity),
    )


def pair_stack(first_is_own, own, other):
    return jnp.stack([jnp.where(first_is_own, own, other), jnp.where(first_is_own, other, own)])


def shards(camera_tiles, tile_block, tile_offset, band_index, interp, psf_taps, background):
    channel = lax.axis_index("by") % 2
    first = channel == 0
    rows = camera_tiles.shape[2]
    table = jnp.concatenate([band_index[:, None].astype(F32), interp.astype(F32)], axis=1)
    table = pair_stack(first, table, swap_pair(table))

    taps = lax.dynamic_index_in_dim(psf_taps, channel, 0, keepdims=False)
    kernels = taps / jnp.sum(taps, axis=1, keepdims=True)
    nx = camera_tiles.shape[4]
    forward, backward = band_matrices(kernels, 2 * rows, Z_DEV, nx)
    backdrop = lax.dynamic_slice_in_dim(background, channel, 1, 0)

    arrived, starts = route_tiles(camera_tiles, tile_block, tile_offset)
    planes, over = gather_planes(arrived, starts)
    blocks = lax.axis_size("bz")
    before = lax.ppermute(over, "bz", [(i, i + 1) for i in range(blocks - 1)])
    table = table.reshape(2 * rows, 3)
    deskewed, *field = deskew(backdrop, table[:, 0].astype(jnp.int32), table[:, 1], table[:, 2], planes, before)

    half = lambda x, start: lax.dynamic_slice_in_dim(x, start, rows, 0)
    other_start = (1 - channel) * rows
    deskewed_other = swap_pair(half(deskewed, other_start))

    estimate = deskewed
    for iteration in range(ITERS):
        halos = halo_exchange(field)
        field = blur_block(True, False, backdrop, field, halos, forward, deskewed)
        halos = halo_exchange(field)
        estimate, *field = blur_block(
            False, iteration == 0, backdrop, field, halos, backward, estimate
        )
    deskewed_out = place_halves(channel, deskewed, deskewed_other)

    theirs = half(estimate, other_start)
    scale = jnp.exp2(jnp.floor(jnp.log2(jnp.max(theirs))) - 13.0)
    got = swap_pair((theirs / scale).astype(jnp.float16)).astype(F32) * swap_pair(scale)
    return deskewed_out, place_halves(channel, estimate, got)


def solution(mesh):
    placed = (P("bz", None, "by", None, None), P(), P(), P("by"), P("by", None), P(), P())
    return jax.shard_map(
        shards,
        mesh=mesh,
        in_specs=placed,
        out_specs=(P(None, "by", "bz", None), P(None, "by", "bz", None)),
        check_vma=False,
    )
```

```python
import functools

import jax
import jax.numpy as jnp
from jax import lax
from jax.experimental import pallas as pl
from jax.experimental.pallas import tpu as pltpu
from jax.sharding import PartitionSpec as P


SHIFT = 8
ITERS = 2
Z_DEV = 64
HALO = 16
SPILL = 2
F32 = jnp.float32
BF16 = jnp.bfloat16


def in_vmem(count):
    return [pl.BlockSpec(memory_space=pltpu.VMEM) for _ in range(count)]


def place_kernel(channel_ref, own_ref, other_ref, out_ref, sems):
    rows = other_ref.shape[0]
    channel = channel_ref[0]
    copies = [
        pltpu.make_async_copy(own_ref.at[pl.ds(channel * rows, rows)], out_ref.at[channel], sems.at[0]),
        pltpu.make_async_copy(other_ref, out_ref.at[1 - channel], sems.at[1]),
    ]
    for copy in copies:
        copy.start()
    for copy in copies:
        copy.wait()


def place_halves(channel, both_rows, other):
    return pl.pallas_call(
        place_kernel,
        out_shape=jax.ShapeDtypeStruct((2,) + other.shape, other.dtype),
        in_specs=[pl.BlockSpec(memory_space=pltpu.SMEM)] + in_vmem(2),
        out_specs=pl.BlockSpec(memory_space=pl.ANY),
        scratch_shapes=[pltpu.SemaphoreType.DMA((2,))],
        compiler_params=pltpu.CompilerParams(vmem_limit_bytes=12 << 20),
        name="place_halves",
    )(channel[None], both_rows, other)


def pack_kernel(own_ref, turn_ref, block_ref, tiles_ref, *rest, base, count):
    *based, spill_ref, seen_ref = rest
    channels, spill = spill_ref.shape[:2]
    blocks = seen_ref.shape[0]
    for block in range(blocks):
        seen_ref[block] = 0

    def place(t, spilled):
        block = block_ref[own_ref[0] * count + t]
        slot = seen_ref[block]
        seen_ref[block] = slot + 1

        if based:

            @pl.when(slot < base)
            def _():
                for c in range(channels):
                    row = (c * blocks + block) * base + slot
                    based[0][row] = jnp.swapaxes(tiles_ref[t, c], 0, 1)

        late = slot >= base

        @pl.when(late & (spilled // spill == turn_ref[0]))
        def _():
            for c in range(channels):
                spill_ref[c, spilled % spill] = jnp.swapaxes(tiles_ref[t, c], 0, 1)

        return spilled + late.astype(jnp.int32)

    lax.fori_loop(0, count, place, 0)


def pack_tiles(camera_tiles, tile_block, turn, base, with_base):
    count, channels, rows, planes, nx = camera_tiles.shape
    blocks = lax.axis_size("bz")
    shape = lambda *lead: jax.ShapeDtypeStruct(lead + (planes, rows, nx), camera_tiles.dtype)
    outs = [shape(channels, SPILL)]
    if with_base:
        outs = [shape(channels * blocks * base)] + outs
    return pl.pallas_call(
        functools.partial(pack_kernel, base=base, count=count),
        out_shape=outs,
        in_specs=[pl.BlockSpec(memory_space=pltpu.SMEM)] * 3 + in_vmem(1),
        out_specs=in_vmem(len(outs)),
        scratch_shapes=[pltpu.SMEM((blocks,), jnp.int32)],
        compiler_params=pltpu.CompilerParams(vmem_limit_bytes=12 << 20),
        name="pack_tiles" if with_base else "pack_spill",
    )(lax.axis_index("bz")[None], turn[None], tile_block, camera_tiles)


def add_tile(planes_ref, here, start, tile):
    for s in range(tile.shape[0]):
        planes_ref[start + s, here, :] += tile[s].astype(F32)


def add_spill(planes_ref, channel_ref, starts_ref, spill_refs):
    for side, spill_ref in enumerate(spill_refs):
        sources, flips, spill, _, rows = spill_ref.shape[:5]
        for m in range(sources):
            for k in range(spill):
                start = starts_ref[(side * sources + m) * spill + k]

                @pl.when(start >= 0)
                def _():
                    for flip in range(flips):
                        half = channel_ref[0] if flip == 0 else 1 - channel_ref[0]
                        here = pl.ds(pl.multiple_of(half * rows, 8), rows)
                        add_tile(planes_ref, here, start, spill_ref[m, flip, k])


def gather_planes_kernel(channel_ref, starts_ref, spill_starts_ref, arrived_ref, one_ref, two_ref, planes_ref, tail_ref):
    halves, slots, _, rows = arrived_ref.shape[:4]
    height = planes_ref.shape[0]

    def clear(z, carry):
        planes_ref[z] = jnp.zeros(planes_ref.shape[1:], F32)
        return carry

    lax.fori_loop(0, height, clear, 0)

    def add(j, carry):
        start = starts_ref[j]

        @pl.when(start >= 0)
        def _():
            for h in range(halves):
                add_tile(planes_ref, pl.ds(h * rows, rows), start, arrived_ref[h, j])

        return carry

    lax.fori_loop(0, slots, add, 0)
    add_spill(planes_ref, channel_ref, spill_starts_ref, (one_ref, two_ref))
    tail_ref[...] = planes_ref[height - tail_ref.shape[0]:]


def gather_planes(channel, starts, spill_starts, arrived, spills):
    halves, _, planes, rows, nx = arrived.shape
    return pl.pallas_call(
        gather_planes_kernel,
        out_shape=[
            jax.ShapeDtypeStruct((Z_DEV + planes - 1, halves * rows, nx), F32),
            jax.ShapeDtypeStruct((SHIFT + planes, halves * rows, nx), F32),
        ],
        in_specs=[pl.BlockSpec(memory_space=pltpu.SMEM)] * 3 + in_vmem(3),
        out_specs=in_vmem(2),
        compiler_params=pltpu.CompilerParams(vmem_limit_bytes=16 << 20),
        name="gather_planes",
    )(channel[None], starts, spill_starts, arrived, *spills)


def more_planes_kernel(channel_ref, spill_starts_ref, one_ref, two_ref, planes_in_ref, planes_ref, tail_ref):
    planes_ref[...] = planes_in_ref[...]
    add_spill(planes_ref, channel_ref, spill_starts_ref, (one_ref, two_ref))
    tail_ref[...] = planes_ref[planes_ref.shape[0] - tail_ref.shape[0]:]


def more_planes(channel, spill_starts, spills, planes, tail):
    return pl.pallas_call(
        more_planes_kernel,
        out_shape=[jax.ShapeDtypeStruct(x.shape, x.dtype) for x in (planes, tail)],
        in_specs=[pl.BlockSpec(memory_space=pltpu.SMEM)] * 2 + in_vmem(3),
        out_specs=in_vmem(2),
        compiler_params=pltpu.CompilerParams(vmem_limit_bytes=24 << 20),
        name="more_planes",
    )(channel[None], spill_starts, *spills, planes)


def deskew_kernel(odd_ref, backdrop_ref, band_ref, near_ref, far_ref, planes_ref, before_ref,
                  out_ref, cast_ref, out_a_ref, out_b_ref, all_ref, *, pitch):
    ny, nz = out_ref.shape[:2]
    reach = before_ref.shape[0]
    ahead = SHIFT + 1
    backdrop = backdrop_ref[0]
    odd = odd_ref[0] == 1
    for z in range(ahead + nz):
        if z < ahead:
            plane = before_ref[z]
        elif z < reach:
            plane = before_ref[z] + planes_ref[z - ahead]
        else:
            plane = planes_ref[z - ahead]
        all_ref[pl.ds(z * pitch, ny), :] = plane

    def row(y, carry):
        first = (ahead - band_ref[y]) * pitch + y
        value = near_ref[y] * all_ref[pl.ds(first, nz, stride=pitch), :]
        value = value + far_ref[y] * all_ref[pl.ds(first - pitch, nz, stride=pitch), :]
        out_ref[y] = value
        cast = (value + backdrop).astype(BF16)
        cast_ref[y] = cast
        bottom, top = cast[:HALO], cast[nz - HALO:]
        out_a_ref[y] = jnp.where(odd, bottom, top)
        out_b_ref[y] = jnp.where(odd, top, bottom)
        return carry

    lax.fori_loop(0, ny, row, 0, unroll=4)


def deskew(backdrop, band, near, far, planes, before):
    ny, nx = planes.shape[1:]
    pitch = ny + 8
    smem = [pl.BlockSpec(memory_space=pltpu.SMEM)] * 5
    return pl.pallas_call(
        functools.partial(deskew_kernel, pitch=pitch),
        out_shape=[
            jax.ShapeDtypeStruct((ny, Z_DEV, nx), F32),
            jax.ShapeDtypeStruct((ny, Z_DEV, nx), BF16),
            jax.ShapeDtypeStruct((ny, HALO, nx), BF16),
            jax.ShapeDtypeStruct((ny, HALO, nx), BF16),
        ],
        in_specs=smem + in_vmem(2),
        out_specs=in_vmem(4),
        scratch_shapes=[pltpu.VMEM(((Z_DEV + SHIFT + 1) * pitch, nx), F32)],
        compiler_params=pltpu.CompilerParams(vmem_limit_bytes=24 << 20),
        name="deskew",
    )(odd_block(), backdrop, band, near, far, planes, before)


def pair_lanes(x, index, height):
    return jnp.concatenate(
        [x[index * height:(index + 1) * height], x[(index + 1) * height:(index + 2) * height]], axis=1
    )


def blur_x(pieces, mx):
    stack = jnp.concatenate(pieces, axis=0)
    return jnp.dot(jnp.concatenate([stack, stack], axis=1), mx, preferred_element_type=F32).astype(BF16)


def three_terms(column):
    head = column.astype(BF16)
    tail = (column - head.astype(F32)).astype(BF16)
    return jnp.concatenate([head, tail, head], axis=0)


def inner_kernel(own_ref, mx_ref, mz_ref, my_ref, out_ref, mid_ref):
    ny, nz, lanes = own_ref.shape
    mx, mz, my = mx_ref[...], mz_ref[...], my_ref[...]
    pitch = nz + 8
    group = 16
    ahead = 8

    def planes(g, carry):
        alongx = blur_x([own_ref[g * group + k] for k in range(group)], mx)
        for k in range(0, group, 4):
            first, second = pair_lanes(alongx, k, nz), pair_lanes(alongx, k + 2, nz)
            both = jnp.dot(
                mz, jnp.concatenate([first, first, second, second], axis=0), preferred_element_type=F32
            )
            row = pl.multiple_of((g * group + k) * pitch, 8)
            mid_ref[pl.ds(row, nz), :] = both[:nz, :lanes]
            mid_ref[pl.ds(row + pitch, nz), :] = both[:nz, lanes:]
            mid_ref[pl.ds(row + 2 * pitch, nz), :] = both[nz:, :lanes]
            mid_ref[pl.ds(row + 3 * pitch, nz), :] = both[nz:, lanes:]
        return carry

    lax.fori_loop(0, ny // group, planes, 0)

    def columns(g, carry):
        for k in range(ahead):
            z = (g * ahead + k) * 2
            terms = [three_terms(mid_ref[pl.ds(z + i, ny, stride=pitch), :]) for i in range(2)]
            both = jnp.dot(my, jnp.concatenate(terms, axis=1), preferred_element_type=F32)
            out_ref[pl.ds(z, ny, stride=pitch), :] = both[:, :lanes]
            out_ref[pl.ds(z + 1, ny, stride=pitch), :] = both[:, lanes:]
        return carry

    lax.fori_loop(0, nz // (2 * ahead), columns, 0)


def outer_kernel(odd_ref, backdrop_ref, inner_ref, a_ref, b_ref, side_ref, side_a_ref, side_b_ref,
                 mx_ref, mze_ref, mzs_ref, mye_ref, mys_ref, point_ref, *rest, quotient, first, ny, nz):
    if quotient:
        cast_ref, out_a_ref, out_b_ref, edge_ref, rim_ref, more_ref = rest
    else:
        full_ref, peak_ref, cast_ref, out_a_ref, out_b_ref, edge_ref, rim_ref, more_ref = rest
    nside = side_ref.shape[0]
    mx, mze, mzs, mye, mys = mx_ref[...], mze_ref[...], mzs_ref[...], mye_ref[...], mys_ref[...]
    lanes = mx.shape[1]
    pitch = nz + 8
    faces = 2 * HALO
    edge_pitch = faces + 8
    width = nz + faces
    group = 16

    def face_planes(g, carry):
        pieces = []
        for k in range(group):
            pieces += [a_ref[g * group + k], b_ref[g * group + k]]
        alongx = blur_x(pieces, mx)
        for k in range(0, group, 8):
            pairs = []
            for p in range(4):
                pairs += [pair_lanes(alongx, k + 2 * p, faces)] * 2
            both = jnp.dot(mze, jnp.concatenate(pairs, axis=0), preferred_element_type=F32)
            for p in range(4):
                row = pl.multiple_of((g * group + k + 2 * p) * edge_pitch, 8)
                edge_ref[pl.ds(row, faces), :] = both[p * faces:(p + 1) * faces, :lanes]
                edge_ref[pl.ds(row + edge_pitch, faces), :] = both[p * faces:(p + 1) * faces, lanes:]
        return carry

    lax.fori_loop(0, ny // group, face_planes, 0)

    for g in range(nside // group):
        pieces = []
        for k in range(group):
            y = g * group + k
            pieces += [side_a_ref[y], side_ref[y], side_b_ref[y]]
        alongx = blur_x(pieces, mx)
        for k in range(0, group, 2):
            pair = pair_lanes(alongx, k, width)
            both = jnp.dot(mzs, jnp.concatenate([pair, pair], axis=0), preferred_element_type=F32)
            row = (g * group + k) * pitch
            rim_ref[pl.ds(row, nz), :] = both[:, :lanes]
            rim_ref[pl.ds(row + pitch, nz), :] = both[:, lanes:]

    def rim(z):
        return rim_ref[pl.ds(z, nside, stride=pitch), :]

    for z in range(0, nz, 2):
        if z < HALO or z >= nz - HALO:
            e = z if z < HALO else z - nz + faces
            terms = [
                three_terms(jnp.concatenate([edge_ref[pl.ds(e + i, ny, stride=edge_pitch), :], rim(z + i)], axis=0))
                for i in range(2)
            ]
            both = jnp.dot(mye, jnp.concatenate(terms, axis=1), preferred_element_type=F32)
        else:
            terms = [three_terms(rim(z + i)) for i in range(2)]
            both = jnp.dot(mys, jnp.concatenate(terms, axis=1), preferred_element_type=F32)
        more_ref[pl.ds(z, ny, stride=pitch), :] = both[:, :lanes]
        more_ref[pl.ds(z + 1, ny, stride=pitch), :] = both[:, lanes:]

    backdrop = backdrop_ref[0]
    odd = odd_ref[0] == 1

    def finish(y, carry):
        row = pl.multiple_of(y * pitch, 8)
        blurred = inner_ref[pl.ds(row, nz), :] + more_ref[pl.ds(row, nz), :]
        if quotient:
            value = point_ref[y] / (blurred + backdrop)
        else:
            value = (point_ref[y] + backdrop if first else point_ref[y]) * blurred
            full_ref[y] = value
            carry = jnp.maximum(carry, value)
        cast = value.astype(BF16)
        cast_ref[y] = cast
        bottom, top = cast[:HALO], cast[nz - HALO:]
        out_a_ref[y] = jnp.where(odd, bottom, top)
        out_b_ref[y] = jnp.where(odd, top, bottom)
        return carry

    peak = lax.fori_loop(0, ny, finish, 0 if quotient else jnp.zeros((nz, lanes), F32), unroll=8)
    if not quotient:
        peak_ref[...] = peak


def blur_inner(block, matrices):
    ny, nz, nx = block.shape
    return pl.pallas_call(
        inner_kernel,
        out_shape=jax.ShapeDtypeStruct((ny * (nz + 8), nx), F32),
        in_specs=in_vmem(4),
        out_specs=in_vmem(1)[0],
        scratch_shapes=[pltpu.VMEM((ny * (nz + 8), nx), F32)],
        compiler_params=pltpu.CompilerParams(vmem_limit_bytes=20 << 20),
        cost_estimate=pl.CostEstimate(flops=20_000_000_000, transcendentals=0, bytes_accessed=8_000_000),
        name="blur_inner",
    )(block, *matrices)


def blur_outer(quotient, first, backdrop, inner, halos, matrices, point):
    ny, nz, nx = point.shape
    nside = halos[2].shape[0]
    outs = [
        jax.ShapeDtypeStruct((ny, nz, nx), BF16),
        jax.ShapeDtypeStruct((ny, HALO, nx), BF16),
        jax.ShapeDtypeStruct((ny, HALO, nx), BF16),
    ]
    if not quotient:
        outs = [jax.ShapeDtypeStruct((ny, nz, nx), F32), jax.ShapeDtypeStruct((nz, nx), F32)] + outs
    return pl.pallas_call(
        functools.partial(outer_kernel, quotient=quotient, first=first, ny=ny, nz=nz),
        out_shape=outs,
        in_specs=[pl.BlockSpec(memory_space=pltpu.SMEM)] * 2 + in_vmem(12),
        out_specs=in_vmem(len(outs)),
        scratch_shapes=[
            pltpu.VMEM((ny * (2 * HALO + 8), nx), F32),
            pltpu.VMEM((nside * (nz + 8), nx), F32),
            pltpu.VMEM((ny * (nz + 8), nx), F32),
        ],
        compiler_params=pltpu.CompilerParams(vmem_limit_bytes=32 << 20),
        cost_estimate=pl.CostEstimate(flops=10_000_000_000, transcendentals=0, bytes_accessed=16_000_000),
        name="blur_quotient" if quotient else "blur_estimate",
    )(odd_block(), backdrop, inner, *halos, *matrices, point)


def odd_block():
    return (lax.axis_index("bz") % 2)[None]


def partners(count):
    phases = [[(i, i ^ 1) for i in range(count)]]
    if count > 2:
        phases.append([(i, ((i + 1) ^ 1) - 1) for i in range(1, count - 1)])
    return phases


def halo_exchange(field):
    block, *faces = field
    rows = block.shape[0]
    blocks = lax.axis_size("bz")
    odd = (lax.axis_index("by") // 2) % 2
    z_phases = partners(blocks)
    ends = [jnp.where(odd == 1, 0, rows - HALO), jnp.where(odd == 1, rows - HALO, 0)]
    sides = []
    corners = [[] for _ in z_phases]
    for start, pairs in zip(ends, partners(lax.axis_size("by") // 2)):
        pairs = [(2 * a + c, 2 * b + c) for a, b in pairs for c in range(2)]
        sides.append(lax.ppermute(lax.dynamic_slice_in_dim(block, start, HALO, 0), "by", pairs))
        for face, z_pairs, found in zip(faces, z_phases, corners):
            both = [(a * blocks + p, b * blocks + q) for a, b in pairs for p, q in z_pairs]
            found.append(lax.ppermute(lax.dynamic_slice_in_dim(face, start, HALO, 0), ("by", "bz"), both))
    across = [lax.ppermute(face, "bz", pairs) for face, pairs in zip(faces, z_phases)]
    join = lambda parts: parts[0] if len(parts) == 1 else jnp.concatenate(parts, axis=0)
    return *across, join(sides), *[join(found) for found in corners]


def head_tail(matrix):
    head = lax.reduce_precision(matrix, 8, 7)
    return head.astype(BF16), (matrix - head).astype(BF16)


def band(taps, out_place, in_place):
    count = taps.shape[0]
    offset = in_place[None, :] - out_place[:, None] + count // 2
    matches = (offset[:, :, None] == jnp.arange(count)[None, None, :]).astype(F32)
    return jnp.einsum("ijw,cw->cij", matches, jnp.stack([taps, taps[::-1]]), precision=lax.Precision.HIGHEST)


def band_matrices(taps, ny, nz, nx):
    near = jnp.arange(HALO)
    odd_y = (lax.axis_index("by") // 2) % 2 == 1
    odd_z = lax.axis_index("bz") % 2 == 1
    sides = [jnp.where(odd_y, near - HALO, near + ny), jnp.where(odd_y, near + ny, near - HALO)]
    sides = sides[: len(partners(lax.axis_size("by") // 2))]
    face_a = jnp.where(odd_z, near - HALO, near + nz)
    face_b = jnp.where(odd_z, near + nz, near - HALO)
    along, depth, height = jnp.arange(nx), jnp.arange(nz), jnp.arange(ny)
    side = jnp.concatenate(sides)
    edge = jnp.concatenate([near, near + nz - HALO])
    face = jnp.concatenate([face_a, face_b])

    def spread(matrix, count):
        eye = jnp.eye(count, dtype=matrix.dtype)[None, :, None, :, None]
        blocks = eye * matrix[:, None, :, None, :]
        return blocks.reshape(2, count * matrix.shape[1], count * matrix.shape[2])

    mx = jnp.concatenate(head_tail(band(taps[2], along, along)[::-1]), axis=1)
    mz = spread(jnp.concatenate(head_tail(band(taps[1], depth, depth)), axis=2), 2)
    mze = spread(jnp.concatenate(head_tail(band(taps[1], edge, face)), axis=2), 4)
    mzs = jnp.concatenate(
        head_tail(band(taps[1], depth, jnp.concatenate([face_a, depth, face_b]))), axis=2
    )

    def three(columns):
        head, tail = head_tail(band(taps[0], height, columns))
        return jnp.concatenate([head, head, tail], axis=2)

    my, mye, mys = three(height), three(jnp.concatenate([height, side])), three(side)
    return [((mx[i], mz[i], my[i]), (mx[i], mze[i], mzs[i], mye[i], mys[i])) for i in range(2)]


def swap_pair(x):
    return lax.ppermute(x, "by", [(i, i ^ 1) for i in range(lax.axis_size("by"))])


def share_spill(spill):
    blocks = lax.axis_size("bz")
    wide = lax.axis_size("by")
    channel = lax.axis_index("by") % 2
    found = []
    for m in range(0, blocks, 2):
        for flip in range(2):
            piece = lax.dynamic_index_in_dim(spill, channel ^ flip, 0, keepdims=False)
            if m or flip:
                pairs = [(b * blocks + z, (b ^ flip) * blocks + (z ^ m)) for b in range(wide) for z in range(blocks)]
                piece = lax.ppermute(piece, ("by", "bz"), pairs)
            found.append(piece)
    line = jnp.stack(found).reshape((blocks // 2, 2) + spill.shape[1:])
    return line, lax.ppermute(line, "bz", [(z, z ^ 1) for z in range(blocks)])


def route_tiles(camera_tiles, tile_block, tile_offset):
    count = camera_tiles.shape[0]
    blocks = lax.axis_size("bz")
    wide = lax.axis_size("by")
    base = max(1, count // blocks)
    own = lax.axis_index("bz")
    channel = lax.axis_index("by") % 2
    named = tile_block[:, 0]
    outgoing, spill = pack_tiles(camera_tiles, named, jnp.int32(0), base, True)
    groups = [
        [(2 * j + c) * blocks + z for c in range(2) for z in range(blocks)] for j in range(wide // 2)
    ]
    arrived = lax.all_to_all(
        outgoing.reshape((2 * blocks, base) + outgoing.shape[1:]),
        ("by", "bz"), split_axis=0, concat_axis=0, axis_index_groups=groups, tiled=True,
    )
    targets = named.reshape(blocks, count)
    offsets = tile_offset.reshape(blocks, count)
    same = (targets[:, :, None] == targets[:, None, :]) & jnp.tri(count, k=-1, dtype=bool)[None]
    places = jnp.sum(same.astype(jnp.int32), axis=2)
    late = places >= base
    order = jnp.sum(jnp.where(late[:, None, :] & jnp.tri(count, k=-1, dtype=bool)[None], 1, 0), axis=2)
    mine = targets == own
    pick = lambda chosen: jnp.sum(jnp.where(chosen, offsets[:, :, None] + 1, 0), axis=1) - 1
    starts = pick(mine[:, :, None] & (places[:, :, None] == jnp.arange(base))).reshape(-1)
    sources = jnp.concatenate([(own ^ core) ^ jnp.arange(0, blocks, 2) for core in range(2)])

    def spill_starts(turn):
        chosen = (mine & late)[:, :, None] & (order[:, :, None] == turn * SPILL + jnp.arange(SPILL))
        return jnp.take(pick(chosen), sources, axis=0, mode="clip").reshape(-1)

    turns = (jnp.max(jnp.sum(late.astype(jnp.int32), axis=1)) + SPILL - 1) // SPILL
    spills = share_spill(spill)
    arrived = arrived.reshape((2, blocks * base) + arrived.shape[2:])
    planes, tail = gather_planes(channel, starts, spill_starts(0), arrived, spills)

    def turn_step(carry):
        turn, planes, tail = carry
        again = pack_tiles(camera_tiles, named, turn, base, False)[0]
        planes, tail = more_planes(channel, spill_starts(turn), share_spill(again), planes, tail)
        return turn + 1, planes, tail

    planes, tail = lax.cond(
        turns > 1,
        lambda planes, tail: lax.while_loop(lambda c: c[0] < turns, turn_step, (jnp.int32(1), planes, tail))[1:],
        lambda planes, tail: (planes, tail),
        planes,
        tail,
    )
    return planes, tail


def pair_stack(first_is_own, own, other):
    return jnp.stack([jnp.where(first_is_own, own, other), jnp.where(first_is_own, other, own)])


def shards(camera_tiles, tile_block, tile_offset, band_index, interp, psf_taps, background):
    channel = lax.axis_index("by") % 2
    first = channel == 0
    rows = camera_tiles.shape[2]
    table = jnp.concatenate([band_index[:, None].astype(F32), interp.astype(F32)], axis=1)
    table = pair_stack(first, table, swap_pair(table))

    taps = lax.dynamic_index_in_dim(psf_taps, channel, 0, keepdims=False)
    kernels = taps / jnp.sum(taps, axis=1, keepdims=True)
    nx = camera_tiles.shape[4]
    forward, backward = band_matrices(kernels, 2 * rows, Z_DEV, nx)
    backdrop = lax.dynamic_slice_in_dim(background, channel, 1, 0)

    planes, over = route_tiles(camera_tiles, tile_block, tile_offset)
    blocks = lax.axis_size("bz")
    before = lax.ppermute(over, "bz", [(i, i + 1) for i in range(blocks - 1)])
    table = table.reshape(2 * rows, 3)
    deskewed, *field = deskew(backdrop, table[:, 0].astype(jnp.int32), table[:, 1], table[:, 2], planes, before)

    half = lambda x, start: lax.dynamic_slice_in_dim(x, start, rows, 0)
    other_start = (1 - channel) * rows
    deskewed_other = swap_pair(half(deskewed, other_start))

    estimate = deskewed
    for iteration in range(ITERS):
        halos = halo_exchange(field)
        inner = blur_inner(field[0], forward[0])
        field = blur_outer(True, False, backdrop, inner, halos, forward[1], deskewed)
        halos = halo_exchange(field)
        inner = blur_inner(field[0], backward[0])
        estimate, peak, *field = blur_outer(
            False, iteration == 0, backdrop, inner, halos, backward[1], estimate
        )
    deskewed_out = place_halves(channel, deskewed, deskewed_other)

    theirs = half(estimate, other_start)
    scale = jnp.exp2(jnp.floor(jnp.log2(jnp.max(peak))) - 13.0)
    got = swap_pair((theirs / scale).astype(jnp.float16)).astype(F32) * swap_pair(scale)
    return deskewed_out, place_halves(channel, estimate, got)


def solution(mesh):
    placed = (P("bz", None, "by", None, None), P(), P(), P("by"), P("by", None), P(), P())
    return jax.shard_map(
        shards,
        mesh=mesh,
        in_specs=placed,
        out_specs=(P(None, "by", "bz", None), P(None, "by", "bz", None)),
        check_vma=False,
    )
```

```python
import functools

import jax
import jax.numpy as jnp
from jax import lax
from jax.experimental import pallas as pl
from jax.experimental.pallas import tpu as pltpu
from jax.sharding import PartitionSpec as P


SHIFT = 8
ITERS = 2
Z_DEV = 64
HALO = 16
SPILL = 2
F32 = jnp.float32
BF16 = jnp.bfloat16


def in_vmem(count):
    return [pl.BlockSpec(memory_space=pltpu.VMEM) for _ in range(count)]


def place_own_kernel(channel_ref, both_ref, out_ref, sem):
    rows = out_ref.shape[1]
    channel = channel_ref[0]
    copy = pltpu.make_async_copy(
        both_ref.at[pl.ds(pl.multiple_of(channel * rows, 8), rows)], out_ref.at[channel], sem
    )
    copy.start()
    copy.wait()


def place_other_kernel(channel_ref, other_ref, partial_ref, out_ref, sem):
    copy = pltpu.make_async_copy(other_ref, out_ref.at[1 - channel_ref[0]], sem)
    copy.start()
    copy.wait()


def place_own(channel, both_rows):
    rows = both_rows.shape[0] // 2
    return pl.pallas_call(
        place_own_kernel,
        out_shape=jax.ShapeDtypeStruct((2, rows) + both_rows.shape[1:], both_rows.dtype),
        in_specs=[pl.BlockSpec(memory_space=pltpu.SMEM)] + in_vmem(1),
        out_specs=pl.BlockSpec(memory_space=pl.ANY),
        scratch_shapes=[pltpu.SemaphoreType.DMA(())],
        compiler_params=pltpu.CompilerParams(vmem_limit_bytes=8 << 20),
        name="place_own",
    )(channel[None], both_rows)


def place_other(channel, other, partial):
    return pl.pallas_call(
        place_other_kernel,
        out_shape=jax.ShapeDtypeStruct(partial.shape, partial.dtype),
        in_specs=[pl.BlockSpec(memory_space=pltpu.SMEM)] + in_vmem(1) + [pl.BlockSpec(memory_space=pl.ANY)],
        out_specs=pl.BlockSpec(memory_space=pl.ANY),
        scratch_shapes=[pltpu.SemaphoreType.DMA(())],
        input_output_aliases={2: 0},
        compiler_params=pltpu.CompilerParams(vmem_limit_bytes=8 << 20),
        name="place_other",
    )(channel[None], other, partial)


def pack_kernel(own_ref, channel_ref, turn_ref, block_ref, tiles_ref, *rest, base, count):
    *based, keep_ref, flip_ref, seen_ref = rest
    channels, spill = tiles_ref.shape[1], keep_ref.shape[0]
    blocks = seen_ref.shape[0]
    for block in range(blocks):
        seen_ref[block] = 0

    def place(t, spilled):
        block = block_ref[own_ref[0] * count + t]
        slot = seen_ref[block]
        seen_ref[block] = slot + 1

        if based:

            @pl.when(slot < base)
            def _():
                for c in range(channels):
                    row = (c * blocks + block) * base + slot
                    based[0][row] = jnp.swapaxes(tiles_ref[t, c], 0, 1)

        late = slot >= base

        @pl.when(late & (spilled // spill == turn_ref[0]))
        def _():
            keep_ref[spilled % spill] = jnp.swapaxes(tiles_ref[t, channel_ref[0]], 0, 1)
            flip_ref[spilled % spill] = jnp.swapaxes(tiles_ref[t, 1 - channel_ref[0]], 0, 1)

        return spilled + late.astype(jnp.int32)

    lax.fori_loop(0, count, place, 0)


def pack_tiles(camera_tiles, tile_block, turn, base, with_base):
    count, channels, rows, planes, nx = camera_tiles.shape
    blocks = lax.axis_size("bz")
    shape = lambda *lead: jax.ShapeDtypeStruct(lead + (planes, rows, nx), camera_tiles.dtype)
    outs = [shape(SPILL), shape(SPILL)]
    if with_base:
        outs = [shape(channels * blocks * base)] + outs
    return pl.pallas_call(
        functools.partial(pack_kernel, base=base, count=count),
        out_shape=outs,
        in_specs=[pl.BlockSpec(memory_space=pltpu.SMEM)] * 4 + in_vmem(1),
        out_specs=in_vmem(len(outs)),
        scratch_shapes=[pltpu.SMEM((blocks,), jnp.int32)],
        compiler_params=pltpu.CompilerParams(vmem_limit_bytes=12 << 20),
        name="pack_tiles" if with_base else "pack_spill",
    )(lax.axis_index("bz")[None], (lax.axis_index("by") % 2)[None], turn[None], tile_block, camera_tiles)


def add_tile(planes_ref, here, start, tile):
    for s in range(tile.shape[0]):
        planes_ref[start + s, here, :] += tile[s].astype(F32)


def add_spill(planes_ref, channel_ref, starts_ref, spill_refs):
    for side, spill_ref in enumerate(spill_refs):
        sources, flips, spill, _, rows = spill_ref.shape[:5]
        for m in range(sources):
            for k in range(spill):
                start = starts_ref[(side * sources + m) * spill + k]

                @pl.when(start >= 0)
                def _():
                    for flip in range(flips):
                        half = channel_ref[0] if flip == 0 else 1 - channel_ref[0]
                        here = pl.ds(pl.multiple_of(half * rows, 8), rows)
                        add_tile(planes_ref, here, start, spill_ref[m, flip, k])


def gather_planes_kernel(channel_ref, starts_ref, spill_starts_ref, arrived_ref, one_ref, two_ref, planes_ref, tail_ref):
    halves, slots, _, rows = arrived_ref.shape[:4]
    height = planes_ref.shape[0]

    def clear(z, carry):
        planes_ref[z] = jnp.zeros(planes_ref.shape[1:], F32)
        return carry

    lax.fori_loop(0, height, clear, 0)

    def add(j, carry):
        start = starts_ref[j]

        @pl.when(start >= 0)
        def _():
            for h in range(halves):
                add_tile(planes_ref, pl.ds(h * rows, rows), start, arrived_ref[h, j])

        return carry

    lax.fori_loop(0, slots, add, 0)
    add_spill(planes_ref, channel_ref, spill_starts_ref, (one_ref, two_ref))
    tail_ref[...] = planes_ref[height - tail_ref.shape[0]:]


def gather_planes(channel, starts, spill_starts, arrived, spills):
    halves, _, planes, rows, nx = arrived.shape
    return pl.pallas_call(
        gather_planes_kernel,
        out_shape=[
            jax.ShapeDtypeStruct((Z_DEV + planes - 1, halves * rows, nx), F32),
            jax.ShapeDtypeStruct((SHIFT + planes, halves * rows, nx), F32),
        ],
        in_specs=[pl.BlockSpec(memory_space=pltpu.SMEM)] * 3 + in_vmem(3),
        out_specs=in_vmem(2),
        compiler_params=pltpu.CompilerParams(vmem_limit_bytes=16 << 20),
        name="gather_planes",
    )(channel[None], starts, spill_starts, arrived, *spills)


def more_planes_kernel(channel_ref, spill_starts_ref, one_ref, two_ref, planes_in_ref, planes_ref, tail_ref):
    planes_ref[...] = planes_in_ref[...]
    add_spill(planes_ref, channel_ref, spill_starts_ref, (one_ref, two_ref))
    tail_ref[...] = planes_ref[planes_ref.shape[0] - tail_ref.shape[0]:]


def more_planes(channel, spill_starts, spills, planes, tail):
    return pl.pallas_call(
        more_planes_kernel,
        out_shape=[jax.ShapeDtypeStruct(x.shape, x.dtype) for x in (planes, tail)],
        in_specs=[pl.BlockSpec(memory_space=pltpu.SMEM)] * 2 + in_vmem(3),
        out_specs=in_vmem(2),
        compiler_params=pltpu.CompilerParams(vmem_limit_bytes=24 << 20),
        name="more_planes",
    )(channel[None], spill_starts, *spills, planes)


def deskew_kernel(odd_ref, backdrop_ref, band_ref, near_ref, far_ref, planes_ref,
                  out_ref, cast_ref, out_a_ref, out_b_ref, all_ref, *, pitch):
    ny, nz = out_ref.shape[:2]
    ahead = SHIFT + 1
    backdrop = backdrop_ref[0]
    odd = odd_ref[0] == 1
    for z in range(ahead):
        all_ref[pl.ds(z * pitch, ny), :] = jnp.zeros((ny, all_ref.shape[1]), F32)
    for z in range(nz):
        all_ref[pl.ds((z + ahead) * pitch, ny), :] = planes_ref[z]

    def row(y, carry):
        first = (ahead - band_ref[y]) * pitch + y
        value = near_ref[y] * all_ref[pl.ds(first, nz, stride=pitch), :]
        value = value + far_ref[y] * all_ref[pl.ds(first - pitch, nz, stride=pitch), :]
        out_ref[y] = value
        cast = (value + backdrop).astype(BF16)
        cast_ref[y] = cast
        bottom, top = cast[:HALO], cast[nz - HALO:]
        out_a_ref[y] = jnp.where(odd, bottom, top)
        out_b_ref[y] = jnp.where(odd, top, bottom)
        return carry

    lax.fori_loop(0, ny, row, 0, unroll=4)


def deskew_more_kernel(odd_ref, backdrop_ref, band_ref, near_ref, far_ref, before_ref,
                       value_ref, cast_in_ref, a_ref, b_ref, out_ref, cast_ref, out_a_ref, out_b_ref, all_ref, *, pitch):
    ny = value_ref.shape[0]
    reach = before_ref.shape[0]
    ahead = SHIFT + 1
    backdrop = backdrop_ref[0]
    odd = odd_ref[0] == 1
    for z in range(ahead + HALO):
        plane = before_ref[z] if z < reach else jnp.zeros(before_ref.shape[1:], F32)
        all_ref[pl.ds(z * pitch, ny), :] = plane

    def row(y, carry):
        first = (ahead - band_ref[y]) * pitch + y
        value = near_ref[y] * all_ref[pl.ds(first, HALO, stride=pitch), :]
        value = value + far_ref[y] * all_ref[pl.ds(first - pitch, HALO, stride=pitch), :]
        value = value + value_ref[y, :HALO]
        out_ref[y, :HALO] = value
        cast = (value + backdrop).astype(BF16)
        cast_ref[y, :HALO] = cast
        out_a_ref[y] = jnp.where(odd, cast, a_ref[y])
        out_b_ref[y] = jnp.where(odd, b_ref[y], cast)
        return carry

    lax.fori_loop(0, ny, row, 0, unroll=8)


def deskew(backdrop, band, near, far, planes):
    ny, nx = planes.shape[1:]
    pitch = ny + 8
    smem = [pl.BlockSpec(memory_space=pltpu.SMEM)] * 5
    return pl.pallas_call(
        functools.partial(deskew_kernel, pitch=pitch),
        out_shape=[
            jax.ShapeDtypeStruct((ny, Z_DEV, nx), F32),
            jax.ShapeDtypeStruct((ny, Z_DEV, nx), BF16),
            jax.ShapeDtypeStruct((ny, HALO, nx), BF16),
            jax.ShapeDtypeStruct((ny, HALO, nx), BF16),
        ],
        in_specs=smem + in_vmem(1),
        out_specs=in_vmem(4),
        scratch_shapes=[pltpu.VMEM(((Z_DEV + SHIFT + 1) * pitch, nx), F32)],
        compiler_params=pltpu.CompilerParams(vmem_limit_bytes=24 << 20),
        cost_estimate=pl.CostEstimate(flops=5_000_000_000, transcendentals=0, bytes_accessed=12_000_000),
        name="deskew",
    )(odd_block(), backdrop, band, near, far, planes)


def deskew_more(backdrop, band, near, far, before, parts):
    ny, nx = before.shape[1:]
    pitch = ny + 8
    smem = [pl.BlockSpec(memory_space=pltpu.SMEM)] * 5
    return pl.pallas_call(
        functools.partial(deskew_more_kernel, pitch=pitch),
        out_shape=[jax.ShapeDtypeStruct(part.shape, part.dtype) for part in parts],
        in_specs=smem + in_vmem(5),
        out_specs=in_vmem(4),
        scratch_shapes=[pltpu.VMEM(((HALO + SHIFT + 1) * pitch, nx), F32)],
        input_output_aliases={6 + i: i for i in range(4)},
        compiler_params=pltpu.CompilerParams(vmem_limit_bytes=16 << 20),
        name="deskew_more",
    )(odd_block(), backdrop, band, near, far, before, *parts)


def pair_lanes(x, index, height):
    return jnp.concatenate(
        [x[index * height:(index + 1) * height], x[(index + 1) * height:(index + 2) * height]], axis=1
    )


def blur_x(pieces, mx):
    stack = jnp.concatenate(pieces, axis=0)
    return jnp.dot(jnp.concatenate([stack, stack], axis=1), mx, preferred_element_type=F32).astype(BF16)


def terms_of(column, coarse):
    head = column.astype(BF16)
    if coarse:
        return jnp.concatenate([head, head], axis=0)
    tail = (column - head.astype(F32)).astype(BF16)
    return jnp.concatenate([head, tail, head], axis=0)


def inner_kernel(own_ref, mx_ref, mz_ref, my_ref, out_ref, mid_ref, *, coarse):
    ny, nz, lanes = own_ref.shape
    pitch = nz + 8
    group = 16
    ahead = 8

    def planes(g, carry):
        mz = mz_ref[...]
        alongx = blur_x([own_ref[g * group + k] for k in range(group)], mx_ref[...])
        for k in range(0, group, 4):
            first, second = pair_lanes(alongx, k, nz), pair_lanes(alongx, k + 2, nz)
            both = jnp.dot(
                mz, jnp.concatenate([first, first, second, second], axis=0), preferred_element_type=F32
            )
            row = pl.multiple_of((g * group + k) * pitch, 8)
            mid_ref[pl.ds(row, nz), :] = both[:nz, :lanes]
            mid_ref[pl.ds(row + pitch, nz), :] = both[:nz, lanes:]
            mid_ref[pl.ds(row + 2 * pitch, nz), :] = both[nz:, :lanes]
            mid_ref[pl.ds(row + 3 * pitch, nz), :] = both[nz:, lanes:]
        return carry

    lax.fori_loop(0, ny // group, planes, 0)

    def columns(g, carry):
        my = my_ref[:, ny:] if coarse else my_ref[...]
        for k in range(ahead):
            z = (g * ahead + k) * 2
            terms = [terms_of(mid_ref[pl.ds(z + i, ny, stride=pitch), :], coarse) for i in range(2)]
            both = jnp.dot(my, jnp.concatenate(terms, axis=1), preferred_element_type=F32)
            out_ref[pl.ds(z, ny, stride=pitch), :] = both[:, :lanes]
            out_ref[pl.ds(z + 1, ny, stride=pitch), :] = both[:, lanes:]
        return carry

    lax.fori_loop(0, nz // (2 * ahead), columns, 0)


def outer_kernel(odd_ref, backdrop_ref, inner_ref, a_ref, b_ref, side_ref, side_a_ref, side_b_ref,
                 mx_ref, mze_ref, mzs_ref, mye_ref, mys_ref, point_ref, *rest, quotient, first, ny, nz):
    if quotient:
        cast_ref, out_a_ref, out_b_ref, edge_ref, rim_ref, more_ref = rest
    else:
        full_ref, peak_ref, cast_ref, out_a_ref, out_b_ref, edge_ref, rim_ref, more_ref = rest
    nside = side_ref.shape[0]
    lanes = mx_ref.shape[1]
    pitch = nz + 8
    faces = 2 * HALO
    edge_pitch = faces + 8
    width = nz + faces
    group = 16

    def face_planes(g, carry):
        pieces = []
        for k in range(group):
            pieces += [a_ref[g * group + k], b_ref[g * group + k]]
        mze = mze_ref[...]
        alongx = blur_x(pieces, mx_ref[...])
        for k in range(0, group, 8):
            pairs = []
            for p in range(4):
                pairs += [pair_lanes(alongx, k + 2 * p, faces)] * 2
            both = jnp.dot(mze, jnp.concatenate(pairs, axis=0), preferred_element_type=F32)
            for p in range(4):
                row = pl.multiple_of((g * group + k + 2 * p) * edge_pitch, 8)
                edge_ref[pl.ds(row, faces), :] = both[p * faces:(p + 1) * faces, :lanes]
                edge_ref[pl.ds(row + edge_pitch, faces), :] = both[p * faces:(p + 1) * faces, lanes:]
        return carry

    lax.fori_loop(0, ny // group, face_planes, 0)

    for g in range(nside // group):
        pieces = []
        for k in range(group):
            y = g * group + k
            pieces += [side_a_ref[y], side_ref[y], side_b_ref[y]]
        alongx = blur_x(pieces, mx_ref[...])
        for k in range(0, group, 2):
            pair = pair_lanes(alongx, k, width)
            both = jnp.dot(mzs_ref[...], jnp.concatenate([pair, pair], axis=0), preferred_element_type=F32)
            row = (g * group + k) * pitch
            rim_ref[pl.ds(row, nz), :] = both[:, :lanes]
            rim_ref[pl.ds(row + pitch, nz), :] = both[:, lanes:]

    def rim(z):
        return rim_ref[pl.ds(z, nside, stride=pitch), :]

    for z in range(0, nz, 2):
        if z < HALO or z >= nz - HALO:
            e = z if z < HALO else z - nz + faces
            terms = [
                terms_of(
                    jnp.concatenate([edge_ref[pl.ds(e + i, ny, stride=edge_pitch), :], rim(z + i)], axis=0), quotient
                )
                for i in range(2)
            ]
            mye = mye_ref[:, ny + nside:] if quotient else mye_ref[...]
            both = jnp.dot(mye, jnp.concatenate(terms, axis=1), preferred_element_type=F32)
        else:
            terms = [terms_of(rim(z + i), quotient) for i in range(2)]
            mys = mys_ref[:, nside:] if quotient else mys_ref[...]
            both = jnp.dot(mys, jnp.concatenate(terms, axis=1), preferred_element_type=F32)
        more_ref[pl.ds(z, ny, stride=pitch), :] = both[:, :lanes]
        more_ref[pl.ds(z + 1, ny, stride=pitch), :] = both[:, lanes:]

    backdrop = backdrop_ref[0]
    odd = odd_ref[0] == 1

    def finish(y, carry):
        row = pl.multiple_of(y * pitch, 8)
        blurred = inner_ref[pl.ds(row, nz), :] + more_ref[pl.ds(row, nz), :]
        if quotient:
            value = point_ref[y] / (blurred + backdrop)
        else:
            value = (point_ref[y] + backdrop if first else point_ref[y]) * blurred
            full_ref[y] = value
            carry = jnp.maximum(carry, value)
        cast = value.astype(BF16)
        cast_ref[y] = cast
        bottom, top = cast[:HALO], cast[nz - HALO:]
        out_a_ref[y] = jnp.where(odd, bottom, top)
        out_b_ref[y] = jnp.where(odd, top, bottom)
        return carry

    peak = lax.fori_loop(0, ny, finish, 0 if quotient else jnp.zeros((nz, lanes), F32), unroll=8)
    if not quotient:
        peak_ref[...] = peak


def blur_inner(coarse, block, matrices):
    ny, nz, nx = block.shape
    return pl.pallas_call(
        functools.partial(inner_kernel, coarse=coarse),
        out_shape=jax.ShapeDtypeStruct((ny * (nz + 8), nx), F32),
        in_specs=in_vmem(4),
        out_specs=in_vmem(1)[0],
        scratch_shapes=[pltpu.VMEM((ny * (nz + 8), nx), F32)],
        compiler_params=pltpu.CompilerParams(vmem_limit_bytes=20 << 20),
        cost_estimate=pl.CostEstimate(flops=20_000_000_000, transcendentals=0, bytes_accessed=8_000_000),
        name="blur_inner",
    )(block, *matrices)


def blur_outer(quotient, first, backdrop, inner, halos, matrices, point):
    ny, nz, nx = point.shape
    nside = halos[2].shape[0]
    outs = [
        jax.ShapeDtypeStruct((ny, nz, nx), BF16),
        jax.ShapeDtypeStruct((ny, HALO, nx), BF16),
        jax.ShapeDtypeStruct((ny, HALO, nx), BF16),
    ]
    if not quotient:
        outs = [jax.ShapeDtypeStruct((ny, nz, nx), F32), jax.ShapeDtypeStruct((nz, nx), F32)] + outs
    return pl.pallas_call(
        functools.partial(outer_kernel, quotient=quotient, first=first, ny=ny, nz=nz),
        out_shape=outs,
        in_specs=[pl.BlockSpec(memory_space=pltpu.SMEM)] * 2 + in_vmem(12),
        out_specs=in_vmem(len(outs)),
        scratch_shapes=[
            pltpu.VMEM((ny * (2 * HALO + 8), nx), F32),
            pltpu.VMEM((nside * (nz + 8), nx), F32),
            pltpu.VMEM((ny * (nz + 8), nx), F32),
        ],
        compiler_params=pltpu.CompilerParams(vmem_limit_bytes=32 << 20),
        cost_estimate=pl.CostEstimate(flops=10_000_000_000, transcendentals=0, bytes_accessed=16_000_000),
        name="blur_quotient" if quotient else "blur_estimate",
    )(odd_block(), backdrop, inner, *halos, *matrices, point)


def odd_block():
    return (lax.axis_index("bz") % 2)[None]


def partners(count):
    phases = [[(i, i ^ 1) for i in range(count)]]
    if count > 2:
        phases.append([(i, ((i + 1) ^ 1) - 1) for i in range(1, count - 1)])
    return phases


def halo_exchange(field):
    block, *faces = field
    rows = block.shape[0]
    blocks = lax.axis_size("bz")
    odd = (lax.axis_index("by") // 2) % 2
    z_phases = partners(blocks)
    ends = [jnp.where(odd == 1, 0, rows - HALO), jnp.where(odd == 1, rows - HALO, 0)]
    sides = []
    corners = [[] for _ in z_phases]
    for start, pairs in zip(ends, partners(lax.axis_size("by") // 2)):
        pairs = [(2 * a + c, 2 * b + c) for a, b in pairs for c in range(2)]
        sides.append(lax.ppermute(lax.dynamic_slice_in_dim(block, start, HALO, 0), "by", pairs))
        for face, z_pairs, found in zip(faces, z_phases, corners):
            both = [(a * blocks + p, b * blocks + q) for a, b in pairs for p, q in z_pairs]
            found.append(lax.ppermute(lax.dynamic_slice_in_dim(face, start, HALO, 0), ("by", "bz"), both))
    across = [lax.ppermute(face, "bz", pairs) for face, pairs in zip(faces, z_phases)]
    join = lambda parts: parts[0] if len(parts) == 1 else jnp.concatenate(parts, axis=0)
    return *across, join(sides), *[join(found) for found in corners]


def cut(index, size, count):
    block = jnp.zeros(index.shape, jnp.int32)
    for k in range(1, count):
        block = block + (index >= k * size).astype(jnp.int32)
    return block, index - block * size


def matrix_kernel(place_ref, taps_ref, *refs, nx, ny, nz, sides):
    count = taps_ref.shape[0] // 3
    odd_y, odd_z = place_ref[0] == 1, place_ref[1] == 1
    face_a = jnp.where(odd_z, -HALO, nz)
    face_b = jnp.where(odd_z, nz, -HALO)
    side_places = [jnp.where(odd_y, -HALO, ny), jnp.where(odd_y, ny, -HALO)][:sides]

    def fill(ref, axis, reverse, places):
        row = lax.broadcasted_iota(jnp.int32, ref.shape, 0)
        lane = lax.broadcasted_iota(jnp.int32, ref.shape, 1)
        offset, tail, kept = places(row, lane)
        offset = offset + count // 2
        matrix = jnp.zeros(ref.shape, F32)
        for t in range(count):
            tap = taps_ref[axis * count + (count - 1 - t if reverse else t)]
            matrix = jnp.where(offset == t, tap, matrix)
        if kept is not None:
            matrix = jnp.where(kept, matrix, 0.0)
        head = matrix.astype(BF16).astype(F32)
        ref[...] = jnp.where(tail, matrix - head, head).astype(BF16)

    def along_x(row, lane):
        part, source = cut(row, nx, 2)
        return source - lane, part == 1, None

    def along_z(row, lane):
        block, out = cut(row, nz, 2)
        lane_block, rest = cut(lane, 2 * nz, 2)
        part, source = cut(rest, nz, 2)
        return source - out, part == 1, block == lane_block

    def face_place(face):
        return jnp.where(face < HALO, face + face_a, face - HALO + face_b)

    def along_edges(row, lane):
        faces = 2 * HALO
        block, edge = cut(row, faces, 4)
        lane_block, rest = cut(lane, 2 * faces, 4)
        part, face = cut(rest, faces, 2)
        out = jnp.where(edge < HALO, edge, edge - faces + nz)
        return face_place(face) - out, part == 1, block == lane_block

    def along_rim(row, lane):
        part, column = cut(lane, nz + 2 * HALO, 2)
        source = jnp.where(
            column < HALO,
            column + face_a,
            jnp.where(column < HALO + nz, column - HALO, column - HALO - nz + face_b),
        )
        return source - row, part == 1, None

    def side_place(column):
        place = column + side_places[0]
        for k in range(1, sides):
            place = jnp.where(column >= k * HALO, column - k * HALO + side_places[k], place)
        return place

    def along_y(row, lane):
        part, column = cut(lane, ny, 3)
        return column - row, part == 2, None

    def along_y_edges(row, lane):
        part, column = cut(lane, ny + sides * HALO, 3)
        source = jnp.where(column < ny, column, side_place(column - ny))
        return source - row, part == 2, None

    def along_y_sides(row, lane):
        part, column = cut(lane, sides * HALO, 3)
        return side_place(column) - row, part == 2, None

    plan = ((2, along_x), (1, along_z), (0, along_y), (1, along_edges), (1, along_rim),
            (0, along_y_edges), (0, along_y_sides))
    for index, (axis, places) in enumerate(plan):
        for turn in range(2):
            fill(refs[turn * len(plan) + index], axis, turn == 1, places)


def band_matrices(kernels, ny, nz, nx):
    place = jnp.stack([(lax.axis_index("by") // 2) % 2, lax.axis_index("bz") % 2])
    sides = len(partners(lax.axis_size("by") // 2))
    shapes = [
        (2 * nx, nx),
        (2 * nz, 4 * nz),
        (ny, 3 * ny),
        (8 * HALO, 16 * HALO),
        (nz, 2 * (nz + 2 * HALO)),
        (ny, 3 * (ny + sides * HALO)),
        (ny, 3 * sides * HALO),
    ]
    found = pl.pallas_call(
        functools.partial(matrix_kernel, nx=nx, ny=ny, nz=nz, sides=sides),
        out_shape=[jax.ShapeDtypeStruct(shape, BF16) for shape in shapes * 2],
        in_specs=[pl.BlockSpec(memory_space=pltpu.SMEM)] * 2,
        out_specs=in_vmem(2 * len(shapes)),
        compiler_params=pltpu.CompilerParams(vmem_limit_bytes=8 << 20),
        name="band_matrices",
    )(place, kernels.reshape(-1))
    turns = [found[: len(shapes)], found[len(shapes):]]
    return [((mx, mz, my), (mx, mze, mzs, mye, mys)) for mx, mz, my, mze, mzs, mye, mys in turns]


def swap_pair(x):
    return lax.ppermute(x, "by", [(i, i ^ 1) for i in range(lax.axis_size("by"))])


def stack_kernel(*refs):
    *parts, out_ref = refs
    for i, part in enumerate(parts):
        out_ref[i] = part[...]


def stack_parts(parts):
    return pl.pallas_call(
        stack_kernel,
        out_shape=jax.ShapeDtypeStruct((len(parts),) + parts[0].shape, parts[0].dtype),
        in_specs=in_vmem(len(parts)),
        out_specs=in_vmem(1)[0],
        compiler_params=pltpu.CompilerParams(vmem_limit_bytes=12 << 20),
        name="stack_parts",
    )(*parts)


def share_spill(spill):
    blocks = lax.axis_size("bz")
    wide = lax.axis_size("by")
    found = []
    for m in range(0, blocks, 2):
        for flip in range(2):
            piece = spill[flip]
            if m or flip:
                pairs = [(b * blocks + z, (b ^ flip) * blocks + (z ^ m)) for b in range(wide) for z in range(blocks)]
                piece = lax.ppermute(piece, ("by", "bz"), pairs)
            found.append(piece)
    line = stack_parts(found)
    line = line.reshape((blocks // 2, 2) + line.shape[1:])
    return line, lax.ppermute(line, "bz", [(z, z ^ 1) for z in range(blocks)])


def route_tiles(camera_tiles, tile_block, tile_offset, prepared):
    count = camera_tiles.shape[0]
    blocks = lax.axis_size("bz")
    wide = lax.axis_size("by")
    base = max(1, count // blocks)
    own = lax.axis_index("bz")
    channel = lax.axis_index("by") % 2
    named = tile_block[:, 0]
    outgoing, *spill = pack_tiles(camera_tiles, named, jnp.int32(0), base, True)
    groups = [
        [(2 * j + c) * blocks + z for c in range(2) for z in range(blocks)] for j in range(wide // 2)
    ]
    arrived = lax.all_to_all(
        outgoing.reshape((2 * blocks, base) + outgoing.shape[1:]),
        ("by", "bz"), split_axis=0, concat_axis=0, axis_index_groups=groups, tiled=True,
    )
    targets = named.reshape(blocks, count)
    offsets = tile_offset.reshape(blocks, count)
    same = (targets[:, :, None] == targets[:, None, :]) & jnp.tri(count, k=-1, dtype=bool)[None]
    places = jnp.sum(same.astype(jnp.int32), axis=2)
    late = places >= base
    order = jnp.sum(jnp.where(late[:, None, :] & jnp.tri(count, k=-1, dtype=bool)[None], 1, 0), axis=2)
    mine = targets == own
    pick = lambda chosen: jnp.sum(jnp.where(chosen, offsets[:, :, None] + 1, 0), axis=1) - 1
    starts = pick(mine[:, :, None] & (places[:, :, None] == jnp.arange(base))).reshape(-1)
    sources = jnp.concatenate([(own ^ core) ^ jnp.arange(0, blocks, 2) for core in range(2)])

    def spill_starts(turn):
        chosen = (mine & late)[:, :, None] & (order[:, :, None] == turn * SPILL + jnp.arange(SPILL))
        return jnp.take(pick(chosen), sources, axis=0, mode="clip").reshape(-1)

    turns = (jnp.max(jnp.sum(late.astype(jnp.int32), axis=1)) + SPILL - 1) // SPILL
    spills = share_spill(spill)
    arrived = arrived.reshape((2, blocks * base) + arrived.shape[2:])
    starts, prepared = lax.optimization_barrier((starts, prepared))
    planes, tail = gather_planes(channel, starts, spill_starts(0), arrived, spills)

    def turn_step(carry):
        turn, planes, tail = carry
        again = pack_tiles(camera_tiles, named, turn, base, False)
        planes, tail = more_planes(channel, spill_starts(turn), share_spill(again), planes, tail)
        return turn + 1, planes, tail

    planes, tail = lax.cond(
        turns > 1,
        lambda planes, tail: lax.while_loop(lambda c: c[0] < turns, turn_step, (jnp.int32(1), planes, tail))[1:],
        lambda planes, tail: (planes, tail),
        planes,
        tail,
    )
    return planes, tail, prepared


def pair_stack(first_is_own, own, other):
    return jnp.stack([jnp.where(first_is_own, own, other), jnp.where(first_is_own, other, own)])


def shards(camera_tiles, tile_block, tile_offset, band_index, interp, psf_taps, background):
    channel = lax.axis_index("by") % 2
    first = channel == 0
    rows = camera_tiles.shape[2]
    table = jnp.concatenate([band_index[:, None].astype(F32), interp.astype(F32)], axis=1)
    table = pair_stack(first, table, swap_pair(table))

    taps = lax.dynamic_index_in_dim(psf_taps, channel, 0, keepdims=False)
    kernels = taps / jnp.sum(taps, axis=1, keepdims=True)
    nx = camera_tiles.shape[4]
    forward, backward = band_matrices(kernels, 2 * rows, Z_DEV, nx)
    backdrop = lax.dynamic_slice_in_dim(background, channel, 1, 0)

    table = table.reshape(2 * rows, 3)
    table = (table[:, 0].astype(jnp.int32), table[:, 1], table[:, 2])
    planes, over, (forward, backward, backdrop, table) = route_tiles(
        camera_tiles, tile_block, tile_offset, (forward, backward, backdrop, table)
    )
    blocks = lax.axis_size("bz")
    before = lax.ppermute(over.astype(jnp.float16), "bz", [(i, i + 1) for i in range(blocks - 1)])
    parts = deskew(backdrop, *table, planes)
    deskewed, *field = deskew_more(backdrop, *table, before.astype(F32), parts)

    half = lambda x, start: lax.dynamic_slice_in_dim(x, start, rows, 0)
    other_start = (1 - channel) * rows
    deskewed_other = swap_pair(half(deskewed, other_start))

    estimate = deskewed
    for iteration in range(ITERS):
        halos = halo_exchange(field)
        inner = blur_inner(True, field[0], forward[0])
        field = blur_outer(True, False, backdrop, inner, halos, forward[1], deskewed)
        halos = halo_exchange(field)
        inner = blur_inner(False, field[0], backward[0])
        estimate, peak, *field = blur_outer(
            False, iteration == 0, backdrop, inner, halos, backward[1], estimate
        )
    theirs = half(estimate, other_start)
    power = jnp.floor(jnp.log2(jnp.max(peak))) - 13.0
    message = jnp.concatenate(
        [theirs * jnp.exp2(-power), jnp.full((1,) + theirs.shape[1:], power)], axis=0
    ).astype(jnp.float16)
    got = swap_pair(message)
    deskewed_out = place_other(channel, deskewed_other, place_own(channel, deskewed))
    partial = place_own(channel, estimate)
    received = got[:rows].astype(F32) * jnp.exp2(got[rows, 0, 0].astype(F32))
    return deskewed_out, place_other(channel, received, partial)


def solution(mesh):
    placed = (P("bz", None, "by", None, None), P(), P(), P("by"), P("by", None), P(), P())
    return jax.shard_map(
        shards,
        mesh=mesh,
        in_specs=placed,
        out_specs=(P(None, "by", "bz", None), P(None, "by", "bz", None)),
        check_vma=False,
    )
```

```python
import functools

import jax
import jax.numpy as jnp
from jax import lax
from jax.experimental import pallas as pl
from jax.experimental.pallas import tpu as pltpu
from jax.sharding import PartitionSpec as P


SHIFT = 8
ITERS = 2
Z_DEV = 64
HALO = 16
SPILL = 2
F32 = jnp.float32
BF16 = jnp.bfloat16


def in_vmem(count):
    return [pl.BlockSpec(memory_space=pltpu.VMEM) for _ in range(count)]


def place_own_kernel(channel_ref, part_ref, both_ref, out_ref, sem):
    rows = out_ref.shape[1]
    channel = channel_ref[0]
    copy = pltpu.make_async_copy(
        both_ref.at[pl.ds(pl.multiple_of(part_ref[0] * rows, 8), rows)], out_ref.at[channel], sem
    )
    copy.start()
    copy.wait()


def place_other_kernel(channel_ref, other_ref, partial_ref, out_ref, sem):
    copy = pltpu.make_async_copy(other_ref, out_ref.at[1 - channel_ref[0]], sem)
    copy.start()
    copy.wait()


def place_own(channel, part, both_rows):
    rows = both_rows.shape[0] // 2
    return pl.pallas_call(
        place_own_kernel,
        out_shape=jax.ShapeDtypeStruct((2, rows) + both_rows.shape[1:], both_rows.dtype),
        in_specs=[pl.BlockSpec(memory_space=pltpu.SMEM)] * 2 + in_vmem(1),
        out_specs=pl.BlockSpec(memory_space=pl.ANY),
        scratch_shapes=[pltpu.SemaphoreType.DMA(())],
        compiler_params=pltpu.CompilerParams(vmem_limit_bytes=8 << 20),
        name="place_own",
    )(channel[None], part[None], both_rows)


def place_other(channel, other, partial):
    return pl.pallas_call(
        place_other_kernel,
        out_shape=jax.ShapeDtypeStruct(partial.shape, partial.dtype),
        in_specs=[pl.BlockSpec(memory_space=pltpu.SMEM)] + in_vmem(1) + [pl.BlockSpec(memory_space=pl.ANY)],
        out_specs=pl.BlockSpec(memory_space=pl.ANY),
        scratch_shapes=[pltpu.SemaphoreType.DMA(())],
        input_output_aliases={2: 0},
        compiler_params=pltpu.CompilerParams(vmem_limit_bytes=8 << 20),
        name="place_other",
    )(channel[None], other, partial)


def pack_kernel(own_ref, channel_ref, turn_ref, block_ref, tiles_ref, *rest, base, count):
    *based, keep_ref, flip_ref, seen_ref = rest
    channels, spill = tiles_ref.shape[1], keep_ref.shape[0]
    blocks = seen_ref.shape[0]
    for block in range(blocks):
        seen_ref[block] = 0

    def place(t, spilled):
        block = block_ref[own_ref[0] * count + t]
        slot = seen_ref[block]
        seen_ref[block] = slot + 1

        if based:

            @pl.when(slot < base)
            def _():
                for c in range(channels):
                    row = (c * blocks + block) * base + slot
                    based[0][row] = jnp.swapaxes(tiles_ref[t, c], 0, 1)

        late = slot >= base

        @pl.when(late & (spilled // spill == turn_ref[0]))
        def _():
            keep_ref[spilled % spill] = jnp.swapaxes(tiles_ref[t, channel_ref[0]], 0, 1)
            flip_ref[spilled % spill] = jnp.swapaxes(tiles_ref[t, 1 - channel_ref[0]], 0, 1)

        return spilled + late.astype(jnp.int32)

    lax.fori_loop(0, count, place, 0)


def pack_tiles(camera_tiles, tile_block, turn, base, with_base):
    count, channels, rows, planes, nx = camera_tiles.shape
    blocks = lax.axis_size("bz")
    shape = lambda *lead: jax.ShapeDtypeStruct(lead + (planes, rows, nx), camera_tiles.dtype)
    outs = [shape(SPILL), shape(SPILL)]
    if with_base:
        outs = [shape(channels * blocks * base)] + outs
    return pl.pallas_call(
        functools.partial(pack_kernel, base=base, count=count),
        out_shape=outs,
        in_specs=[pl.BlockSpec(memory_space=pltpu.SMEM)] * 4 + in_vmem(1),
        out_specs=in_vmem(len(outs)),
        scratch_shapes=[pltpu.SMEM((blocks,), jnp.int32)],
        compiler_params=pltpu.CompilerParams(vmem_limit_bytes=12 << 20),
        name="pack_tiles" if with_base else "pack_spill",
    )(lax.axis_index("bz")[None], (lax.axis_index("by") % 2)[None], turn[None], tile_block, camera_tiles)


def add_tile(planes_ref, here, start, tile):
    for s in range(tile.shape[0]):
        planes_ref[start + s, here, :] += tile[s].astype(F32)


def add_spill(planes_ref, channel_ref, starts_ref, spill_refs):
    for side, spill_ref in enumerate(spill_refs):
        sources, flips, spill, _, rows = spill_ref.shape[:5]
        for m in range(sources):
            for k in range(spill):
                start = starts_ref[(side * sources + m) * spill + k]

                @pl.when(start >= 0)
                def _():
                    for flip in range(flips):
                        half = channel_ref[0] if flip == 0 else 1 - channel_ref[0]
                        here = pl.ds(pl.multiple_of(half * rows, 8), rows)
                        add_tile(planes_ref, here, start, spill_ref[m, flip, k])


def gather_planes_kernel(channel_ref, starts_ref, spill_starts_ref, arrived_ref, one_ref, two_ref, planes_ref, tail_ref):
    halves, slots, _, rows = arrived_ref.shape[:4]
    height = planes_ref.shape[0]

    def clear(z, carry):
        planes_ref[z] = jnp.zeros(planes_ref.shape[1:], F32)
        return carry

    lax.fori_loop(0, height, clear, 0)

    def add(j, carry):
        start = starts_ref[j]

        @pl.when(start >= 0)
        def _():
            for h in range(halves):
                add_tile(planes_ref, pl.ds(h * rows, rows), start, arrived_ref[h, j])

        return carry

    lax.fori_loop(0, slots, add, 0)
    add_spill(planes_ref, channel_ref, spill_starts_ref, (one_ref, two_ref))
    tail_ref[...] = planes_ref[height - tail_ref.shape[0]:]


def gather_planes(channel, starts, spill_starts, arrived, spills):
    halves, _, planes, rows, nx = arrived.shape
    return pl.pallas_call(
        gather_planes_kernel,
        out_shape=[
            jax.ShapeDtypeStruct((Z_DEV + planes - 1, halves * rows, nx), F32),
            jax.ShapeDtypeStruct((SHIFT + planes, halves * rows, nx), F32),
        ],
        in_specs=[pl.BlockSpec(memory_space=pltpu.SMEM)] * 3 + in_vmem(3),
        out_specs=in_vmem(2),
        compiler_params=pltpu.CompilerParams(vmem_limit_bytes=16 << 20),
        name="gather_planes",
    )(channel[None], starts, spill_starts, arrived, *spills)


def more_planes_kernel(channel_ref, spill_starts_ref, one_ref, two_ref, planes_in_ref, planes_ref, tail_ref):
    planes_ref[...] = planes_in_ref[...]
    add_spill(planes_ref, channel_ref, spill_starts_ref, (one_ref, two_ref))
    tail_ref[...] = planes_ref[planes_ref.shape[0] - tail_ref.shape[0]:]


def more_planes(channel, spill_starts, spills, planes, tail):
    return pl.pallas_call(
        more_planes_kernel,
        out_shape=[jax.ShapeDtypeStruct(x.shape, x.dtype) for x in (planes, tail)],
        in_specs=[pl.BlockSpec(memory_space=pltpu.SMEM)] * 2 + in_vmem(3),
        out_specs=in_vmem(2),
        compiler_params=pltpu.CompilerParams(vmem_limit_bytes=24 << 20),
        name="more_planes",
    )(channel[None], spill_starts, *spills, planes)


def deskew_kernel(odd_ref, backdrop_ref, band_ref, near_ref, far_ref, planes_ref,
                  out_ref, cast_ref, out_a_ref, out_b_ref, all_ref, *, pitch):
    ny, nz = out_ref.shape[:2]
    ahead = SHIFT + 1
    backdrop = backdrop_ref[0]
    odd = odd_ref[0] == 1
    for z in range(ahead):
        all_ref[pl.ds(z * pitch, ny), :] = jnp.zeros((ny, all_ref.shape[1]), F32)
    for z in range(nz):
        all_ref[pl.ds((z + ahead) * pitch, ny), :] = planes_ref[z]

    def row(y, carry):
        first = (ahead - band_ref[y]) * pitch + y
        value = near_ref[y] * all_ref[pl.ds(first, nz, stride=pitch), :]
        value = value + far_ref[y] * all_ref[pl.ds(first - pitch, nz, stride=pitch), :]
        out_ref[y] = value
        cast = (value + backdrop).astype(BF16)
        cast_ref[y] = cast
        bottom, top = cast[:HALO], cast[nz - HALO:]
        out_a_ref[y] = jnp.where(odd, bottom, top)
        out_b_ref[y] = jnp.where(odd, top, bottom)
        return carry

    lax.fori_loop(0, ny, row, 0, unroll=4)


def deskew_more_kernel(odd_ref, backdrop_ref, band_ref, near_ref, far_ref, before_ref,
                       value_ref, cast_in_ref, a_ref, b_ref, out_ref, cast_ref, out_a_ref, out_b_ref, all_ref, *, pitch):
    ny = value_ref.shape[0]
    reach = before_ref.shape[0]
    ahead = SHIFT + 1
    backdrop = backdrop_ref[0]
    odd = odd_ref[0] == 1
    for z in range(ahead + HALO):
        plane = before_ref[z] if z < reach else jnp.zeros(before_ref.shape[1:], F32)
        all_ref[pl.ds(z * pitch, ny), :] = plane

    def row(y, carry):
        first = (ahead - band_ref[y]) * pitch + y
        value = near_ref[y] * all_ref[pl.ds(first, HALO, stride=pitch), :]
        value = value + far_ref[y] * all_ref[pl.ds(first - pitch, HALO, stride=pitch), :]
        value = value + value_ref[y, :HALO]
        out_ref[y, :HALO] = value
        cast = (value + backdrop).astype(BF16)
        cast_ref[y, :HALO] = cast
        out_a_ref[y] = jnp.where(odd, cast, a_ref[y])
        out_b_ref[y] = jnp.where(odd, b_ref[y], cast)
        return carry

    lax.fori_loop(0, ny, row, 0, unroll=8)


def deskew(backdrop, band, near, far, planes):
    ny, nx = planes.shape[1:]
    pitch = ny + 8
    smem = [pl.BlockSpec(memory_space=pltpu.SMEM)] * 5
    return pl.pallas_call(
        functools.partial(deskew_kernel, pitch=pitch),
        out_shape=[
            jax.ShapeDtypeStruct((ny, Z_DEV, nx), F32),
            jax.ShapeDtypeStruct((ny, Z_DEV, nx), BF16),
            jax.ShapeDtypeStruct((ny, HALO, nx), BF16),
            jax.ShapeDtypeStruct((ny, HALO, nx), BF16),
        ],
        in_specs=smem + in_vmem(1),
        out_specs=in_vmem(4),
        scratch_shapes=[pltpu.VMEM(((Z_DEV + SHIFT + 1) * pitch, nx), F32)],
        compiler_params=pltpu.CompilerParams(vmem_limit_bytes=24 << 20),
        cost_estimate=pl.CostEstimate(flops=5_000_000_000, transcendentals=0, bytes_accessed=12_000_000),
        name="deskew",
    )(odd_block(), backdrop, band, near, far, planes)


def deskew_more(backdrop, band, near, far, before, parts):
    ny, nx = before.shape[1:]
    pitch = ny + 8
    smem = [pl.BlockSpec(memory_space=pltpu.SMEM)] * 5
    return pl.pallas_call(
        functools.partial(deskew_more_kernel, pitch=pitch),
        out_shape=[jax.ShapeDtypeStruct(part.shape, part.dtype) for part in parts],
        in_specs=smem + in_vmem(5),
        out_specs=in_vmem(4),
        scratch_shapes=[pltpu.VMEM(((HALO + SHIFT + 1) * pitch, nx), F32)],
        input_output_aliases={6 + i: i for i in range(4)},
        compiler_params=pltpu.CompilerParams(vmem_limit_bytes=16 << 20),
        name="deskew_more",
    )(odd_block(), backdrop, band, near, far, before, *parts)


def pair_lanes(x, index, height):
    return jnp.concatenate(
        [x[index * height:(index + 1) * height], x[(index + 1) * height:(index + 2) * height]], axis=1
    )


def blur_x(pieces, mx):
    stack = jnp.concatenate(pieces, axis=0)
    return jnp.dot(jnp.concatenate([stack, stack], axis=1), mx, preferred_element_type=F32).astype(BF16)


def terms_of(column, coarse):
    head = column.astype(BF16)
    if coarse:
        return jnp.concatenate([head, head], axis=0)
    tail = (column - head.astype(F32)).astype(BF16)
    return jnp.concatenate([head, tail, head], axis=0)


def inner_kernel(own_ref, mx_ref, mz_ref, my_ref, out_ref, mid_ref, *, coarse):
    ny, nz, lanes = own_ref.shape
    pitch = nz + 8
    group = ny // 2
    ahead = 16

    def planes(g, carry):
        mz = mz_ref[...]
        alongx = blur_x([own_ref[g * group + k] for k in range(group)], mx_ref[...])
        for k in range(0, group, 4):
            first, second = pair_lanes(alongx, k, nz), pair_lanes(alongx, k + 2, nz)
            both = jnp.dot(
                mz, jnp.concatenate([first, first, second, second], axis=0), preferred_element_type=F32
            )
            row = pl.multiple_of((g * group + k) * pitch, 8)
            mid_ref[pl.ds(row, nz), :] = both[:nz, :lanes]
            mid_ref[pl.ds(row + pitch, nz), :] = both[:nz, lanes:]
            mid_ref[pl.ds(row + 2 * pitch, nz), :] = both[nz:, :lanes]
            mid_ref[pl.ds(row + 3 * pitch, nz), :] = both[nz:, lanes:]
        return carry

    lax.fori_loop(0, ny // group, planes, 0)

    def columns(g, carry):
        my = my_ref[:, ny:] if coarse else my_ref[...]
        for k in range(ahead):
            z = (g * ahead + k) * 2
            terms = [terms_of(mid_ref[pl.ds(z + i, ny, stride=pitch), :], coarse) for i in range(2)]
            both = jnp.dot(my, jnp.concatenate(terms, axis=1), preferred_element_type=F32)
            out_ref[pl.ds(z, ny, stride=pitch), :] = both[:, :lanes]
            out_ref[pl.ds(z + 1, ny, stride=pitch), :] = both[:, lanes:]
        return carry

    lax.fori_loop(0, nz // (2 * ahead), columns, 0)


def outer_kernel(odd_ref, swap_ref, backdrop_ref, inner_ref, a_ref, b_ref, side_ref, side_a_ref, side_b_ref,
                 mx_ref, mze_ref, mzs_ref, mye_ref, mys_ref, point_ref, *rest, quotient, first, ny, nz):
    if quotient:
        cast_ref, out_a_ref, out_b_ref, edge_ref, rim_ref, more_ref = rest
    else:
        full_ref, peak_ref, cast_ref, out_a_ref, out_b_ref, edge_ref, rim_ref, more_ref = rest
    nside = side_ref.shape[0]
    lanes = mx_ref.shape[1]
    pitch = nz + 8
    faces = 2 * HALO
    edge_pitch = faces + 8
    width = nz + faces
    many = ny // 2

    def face_planes(g, carry):
        pieces = []
        for k in range(many):
            pieces += [a_ref[g * many + k], b_ref[g * many + k]]
        mze = mze_ref[...]
        alongx = blur_x(pieces, mx_ref[...])
        for k in range(0, many, 8):
            pairs = []
            for p in range(4):
                pairs += [pair_lanes(alongx, k + 2 * p, faces)] * 2
            both = jnp.dot(mze, jnp.concatenate(pairs, axis=0), preferred_element_type=F32)
            for p in range(4):
                row = pl.multiple_of((g * many + k + 2 * p) * edge_pitch, 8)
                edge_ref[pl.ds(row, faces), :] = both[p * faces:(p + 1) * faces, :lanes]
                edge_ref[pl.ds(row + edge_pitch, faces), :] = both[p * faces:(p + 1) * faces, lanes:]
        return carry

    lax.fori_loop(0, ny // many, face_planes, 0)
    group = 16

    for g in range(nside // group):
        pieces = []
        for k in range(group):
            y = g * group + k
            pieces += [side_a_ref[y], side_ref[y], side_b_ref[y]]
        alongx = blur_x(pieces, mx_ref[...])
        for k in range(0, group, 2):
            pair = pair_lanes(alongx, k, width)
            both = jnp.dot(mzs_ref[...], jnp.concatenate([pair, pair], axis=0), preferred_element_type=F32)
            row = (g * group + k) * pitch
            rim_ref[pl.ds(row, nz), :] = both[:, :lanes]
            rim_ref[pl.ds(row + pitch, nz), :] = both[:, lanes:]

    def rim(z):
        return rim_ref[pl.ds(z, nside, stride=pitch), :]

    for z in range(0, nz, 2):
        if z < HALO or z >= nz - HALO:
            e = z if z < HALO else z - nz + faces
            terms = [
                terms_of(
                    jnp.concatenate([edge_ref[pl.ds(e + i, ny, stride=edge_pitch), :], rim(z + i)], axis=0), quotient
                )
                for i in range(2)
            ]
            mye = mye_ref[:, ny + nside:] if quotient else mye_ref[...]
            both = jnp.dot(mye, jnp.concatenate(terms, axis=1), preferred_element_type=F32)
        else:
            terms = [terms_of(rim(z + i), quotient) for i in range(2)]
            mys = mys_ref[:, nside:] if quotient else mys_ref[...]
            both = jnp.dot(mys, jnp.concatenate(terms, axis=1), preferred_element_type=F32)
        more_ref[pl.ds(z, ny, stride=pitch), :] = both[:, :lanes]
        more_ref[pl.ds(z + 1, ny, stride=pitch), :] = both[:, lanes:]

    backdrop = backdrop_ref[0]
    odd = odd_ref[0] == 1
    swap = swap_ref[0]

    def finish(y, carry):
        row = pl.multiple_of(y * pitch, 8)
        blurred = inner_ref[pl.ds(row, nz), :] + more_ref[pl.ds(row, nz), :]
        if quotient:
            value = point_ref[y] / (blurred + backdrop)
        else:
            value = (point_ref[y] + backdrop if first else point_ref[y]) * blurred
            full_ref[y ^ swap] = value
            carry = jnp.maximum(carry, value)
        cast = value.astype(BF16)
        cast_ref[y] = cast
        bottom, top = cast[:HALO], cast[nz - HALO:]
        out_a_ref[y] = jnp.where(odd, bottom, top)
        out_b_ref[y] = jnp.where(odd, top, bottom)
        return carry

    peak = lax.fori_loop(0, ny, finish, 0 if quotient else jnp.zeros((nz, lanes), F32), unroll=8)
    if not quotient:
        peak_ref[...] = peak


def blur_inner(coarse, block, matrices):
    ny, nz, nx = block.shape
    return pl.pallas_call(
        functools.partial(inner_kernel, coarse=coarse),
        out_shape=jax.ShapeDtypeStruct((ny * (nz + 8), nx), F32),
        in_specs=in_vmem(4),
        out_specs=in_vmem(1)[0],
        scratch_shapes=[pltpu.VMEM((ny * (nz + 8), nx), F32)],
        compiler_params=pltpu.CompilerParams(vmem_limit_bytes=20 << 20),
        cost_estimate=pl.CostEstimate(flops=20_000_000_000, transcendentals=0, bytes_accessed=8_000_000),
        name="blur_inner",
    )(block, *matrices)


def blur_outer(quotient, first, swap, backdrop, inner, halos, matrices, point):
    ny, nz, nx = point.shape
    nside = halos[2].shape[0]
    outs = [
        jax.ShapeDtypeStruct((ny, nz, nx), BF16),
        jax.ShapeDtypeStruct((ny, HALO, nx), BF16),
        jax.ShapeDtypeStruct((ny, HALO, nx), BF16),
    ]
    if not quotient:
        outs = [jax.ShapeDtypeStruct((ny, nz, nx), F32), jax.ShapeDtypeStruct((nz, nx), F32)] + outs
    return pl.pallas_call(
        functools.partial(outer_kernel, quotient=quotient, first=first, ny=ny, nz=nz),
        out_shape=outs,
        in_specs=[pl.BlockSpec(memory_space=pltpu.SMEM)] * 3 + in_vmem(12),
        out_specs=in_vmem(len(outs)),
        scratch_shapes=[
            pltpu.VMEM((ny * (2 * HALO + 8), nx), F32),
            pltpu.VMEM((nside * (nz + 8), nx), F32),
            pltpu.VMEM((ny * (nz + 8), nx), F32),
        ],
        compiler_params=pltpu.CompilerParams(vmem_limit_bytes=32 << 20),
        cost_estimate=pl.CostEstimate(flops=10_000_000_000, transcendentals=0, bytes_accessed=16_000_000),
        name="blur_quotient" if quotient else "blur_estimate",
    )(odd_block(), swap[None], backdrop, inner, *halos, *matrices, point)


def odd_block():
    return (lax.axis_index("bz") % 2)[None]


def partners(count):
    phases = [[(i, i ^ 1) for i in range(count)]]
    if count > 2:
        phases.append([(i, ((i + 1) ^ 1) - 1) for i in range(1, count - 1)])
    return phases


def halo_exchange(field):
    block, *faces = field
    rows = block.shape[0]
    blocks = lax.axis_size("bz")
    odd = (lax.axis_index("by") // 2) % 2
    z_phases = partners(blocks)
    ends = [jnp.where(odd == 1, 0, rows - HALO), jnp.where(odd == 1, rows - HALO, 0)]
    sides = []
    corners = [[] for _ in z_phases]
    across = []
    for face, z_pairs in zip(faces, z_phases):
        across.append(lax.ppermute(face, "bz", z_pairs))
    for start, pairs in zip(ends, partners(lax.axis_size("by") // 2)):
        pairs = [(2 * a + c, 2 * b + c) for a, b in pairs for c in range(2)]
        sides.append(lax.ppermute(lax.dynamic_slice_in_dim(block, start, HALO, 0), "by", pairs))
        for face, z_pairs, found in zip(faces, z_phases, corners):
            both = [(a * blocks + p, b * blocks + q) for a, b in pairs for p, q in z_pairs]
            found.append(lax.ppermute(lax.dynamic_slice_in_dim(face, start, HALO, 0), ("by", "bz"), both))
    join = lambda parts: parts[0] if len(parts) == 1 else jnp.concatenate(parts, axis=0)
    return *across, join(sides), *[join(found) for found in corners]


def cut(index, size, count):
    block = jnp.zeros(index.shape, jnp.int32)
    for k in range(1, count):
        block = block + (index >= k * size).astype(jnp.int32)
    return block, index - block * size


def matrix_kernel(place_ref, taps_ref, *refs, nx, ny, nz, sides):
    count = taps_ref.shape[0] // 3
    odd_y, odd_z = place_ref[0] == 1, place_ref[1] == 1
    face_a = jnp.where(odd_z, -HALO, nz)
    face_b = jnp.where(odd_z, nz, -HALO)
    side_places = [jnp.where(odd_y, -HALO, ny), jnp.where(odd_y, ny, -HALO)][:sides]

    def fill(ref, axis, reverse, places):
        row = lax.broadcasted_iota(jnp.int32, ref.shape, 0)
        lane = lax.broadcasted_iota(jnp.int32, ref.shape, 1)
        offset, tail, kept = places(row, lane)
        offset = offset + count // 2
        matrix = jnp.zeros(ref.shape, F32)
        for t in range(count):
            tap = taps_ref[axis * count + (count - 1 - t if reverse else t)]
            matrix = jnp.where(offset == t, tap, matrix)
        if kept is not None:
            matrix = jnp.where(kept, matrix, 0.0)
        head = matrix.astype(BF16).astype(F32)
        ref[...] = jnp.where(tail, matrix - head, head).astype(BF16)

    def along_x(row, lane):
        part, source = cut(row, nx, 2)
        return source - lane, part == 1, None

    def along_z(row, lane):
        block, out = cut(row, nz, 2)
        lane_block, rest = cut(lane, 2 * nz, 2)
        part, source = cut(rest, nz, 2)
        return source - out, part == 1, block == lane_block

    def face_place(face):
        return jnp.where(face < HALO, face + face_a, face - HALO + face_b)

    def along_edges(row, lane):
        faces = 2 * HALO
        block, edge = cut(row, faces, 4)
        lane_block, rest = cut(lane, 2 * faces, 4)
        part, face = cut(rest, faces, 2)
        out = jnp.where(edge < HALO, edge, edge - faces + nz)
        return face_place(face) - out, part == 1, block == lane_block

    def along_rim(row, lane):
        part, column = cut(lane, nz + 2 * HALO, 2)
        source = jnp.where(
            column < HALO,
            column + face_a,
            jnp.where(column < HALO + nz, column - HALO, column - HALO - nz + face_b),
        )
        return source - row, part == 1, None

    def side_place(column):
        place = column + side_places[0]
        for k in range(1, sides):
            place = jnp.where(column >= k * HALO, column - k * HALO + side_places[k], place)
        return place

    def along_y(row, lane):
        part, column = cut(lane, ny, 3)
        return column - row, part == 2, None

    def along_y_edges(row, lane):
        part, column = cut(lane, ny + sides * HALO, 3)
        source = jnp.where(column < ny, column, side_place(column - ny))
        return source - row, part == 2, None

    def along_y_sides(row, lane):
        part, column = cut(lane, sides * HALO, 3)
        return side_place(column) - row, part == 2, None

    plan = ((2, along_x), (1, along_z), (0, along_y), (1, along_edges), (1, along_rim),
            (0, along_y_edges), (0, along_y_sides))
    for index, (axis, places) in enumerate(plan):
        for turn in range(2):
            fill(refs[turn * len(plan) + index], axis, turn == 1, places)


def band_matrices(kernels, ny, nz, nx):
    place = jnp.stack([(lax.axis_index("by") // 2) % 2, lax.axis_index("bz") % 2])
    sides = len(partners(lax.axis_size("by") // 2))
    shapes = [
        (2 * nx, nx),
        (2 * nz, 4 * nz),
        (ny, 3 * ny),
        (8 * HALO, 16 * HALO),
        (nz, 2 * (nz + 2 * HALO)),
        (ny, 3 * (ny + sides * HALO)),
        (ny, 3 * sides * HALO),
    ]
    found = pl.pallas_call(
        functools.partial(matrix_kernel, nx=nx, ny=ny, nz=nz, sides=sides),
        out_shape=[jax.ShapeDtypeStruct(shape, BF16) for shape in shapes * 2],
        in_specs=[pl.BlockSpec(memory_space=pltpu.SMEM)] * 2,
        out_specs=in_vmem(2 * len(shapes)),
        compiler_params=pltpu.CompilerParams(vmem_limit_bytes=8 << 20),
        name="band_matrices",
    )(place, kernels.reshape(-1))
    turns = [found[: len(shapes)], found[len(shapes):]]
    return [((mx, mz, my), (mx, mze, mzs, mye, mys)) for mx, mz, my, mze, mzs, mye, mys in turns]


def swap_pair(x):
    return lax.ppermute(x, "by", [(i, i ^ 1) for i in range(lax.axis_size("by"))])


def stack_kernel(*refs):
    *parts, out_ref = refs
    for i, part in enumerate(parts):
        out_ref[i] = part[...]


def stack_parts(parts):
    return pl.pallas_call(
        stack_kernel,
        out_shape=jax.ShapeDtypeStruct((len(parts),) + parts[0].shape, parts[0].dtype),
        in_specs=in_vmem(len(parts)),
        out_specs=in_vmem(1)[0],
        compiler_params=pltpu.CompilerParams(vmem_limit_bytes=12 << 20),
        name="stack_parts",
    )(*parts)


def share_spill(spill):
    blocks = lax.axis_size("bz")
    wide = lax.axis_size("by")
    found = []
    for m in range(0, blocks, 2):
        for flip in range(2):
            piece = spill[flip]
            if m or flip:
                pairs = [(b * blocks + z, (b ^ flip) * blocks + (z ^ m)) for b in range(wide) for z in range(blocks)]
                piece = lax.ppermute(piece, ("by", "bz"), pairs)
            found.append(piece)
    line = stack_parts(found)
    line = line.reshape((blocks // 2, 2) + line.shape[1:])
    return line, lax.ppermute(line, "bz", [(z, z ^ 1) for z in range(blocks)])


def route_tiles(camera_tiles, tile_block, tile_offset, prepared):
    count = camera_tiles.shape[0]
    blocks = lax.axis_size("bz")
    wide = lax.axis_size("by")
    base = max(1, count // blocks)
    own = lax.axis_index("bz")
    channel = lax.axis_index("by") % 2
    named = tile_block[:, 0]
    outgoing, *spill = pack_tiles(camera_tiles, named, jnp.int32(0), base, True)
    groups = [
        [(2 * j + c) * blocks + z for c in range(2) for z in range(blocks)] for j in range(wide // 2)
    ]
    arrived = lax.all_to_all(
        outgoing.reshape((2 * blocks, base) + outgoing.shape[1:]),
        ("by", "bz"), split_axis=0, concat_axis=0, axis_index_groups=groups, tiled=True,
    )
    targets = named.reshape(blocks, count)
    offsets = tile_offset.reshape(blocks, count)
    same = (targets[:, :, None] == targets[:, None, :]) & jnp.tri(count, k=-1, dtype=bool)[None]
    places = jnp.sum(same.astype(jnp.int32), axis=2)
    late = places >= base
    order = jnp.sum(jnp.where(late[:, None, :] & jnp.tri(count, k=-1, dtype=bool)[None], 1, 0), axis=2)
    mine = targets == own
    pick = lambda chosen: jnp.sum(jnp.where(chosen, offsets[:, :, None] + 1, 0), axis=1) - 1
    starts = pick(mine[:, :, None] & (places[:, :, None] == jnp.arange(base))).reshape(-1)
    sources = jnp.concatenate([(own ^ core) ^ jnp.arange(0, blocks, 2) for core in range(2)])

    def spill_starts(turn):
        chosen = (mine & late)[:, :, None] & (order[:, :, None] == turn * SPILL + jnp.arange(SPILL))
        return jnp.take(pick(chosen), sources, axis=0, mode="clip").reshape(-1)

    turns = (jnp.max(jnp.sum(late.astype(jnp.int32), axis=1)) + SPILL - 1) // SPILL
    spills = share_spill(spill)
    arrived = arrived.reshape((2, blocks * base) + arrived.shape[2:])
    starts, prepared = lax.optimization_barrier((starts, prepared))
    planes, tail = gather_planes(channel, starts, spill_starts(0), arrived, spills)

    def turn_step(carry):
        turn, planes, tail = carry
        again = pack_tiles(camera_tiles, named, turn, base, False)
        planes, tail = more_planes(channel, spill_starts(turn), share_spill(again), planes, tail)
        return turn + 1, planes, tail

    planes, tail = lax.cond(
        turns > 1,
        lambda planes, tail: lax.while_loop(lambda c: c[0] < turns, turn_step, (jnp.int32(1), planes, tail))[1:],
        lambda planes, tail: (planes, tail),
        planes,
        tail,
    )
    return planes, tail, prepared


def pair_stack(first_is_own, own, other):
    return jnp.stack([jnp.where(first_is_own, own, other), jnp.where(first_is_own, other, own)])


def shards(camera_tiles, tile_block, tile_offset, band_index, interp, psf_taps, background):
    channel = lax.axis_index("by") % 2
    first = channel == 0
    rows = camera_tiles.shape[2]
    table = jnp.concatenate([band_index[:, None].astype(F32), interp.astype(F32)], axis=1)
    table = pair_stack(first, table, swap_pair(table))

    taps = lax.dynamic_index_in_dim(psf_taps, channel, 0, keepdims=False)
    kernels = taps / jnp.sum(taps, axis=1, keepdims=True)
    nx = camera_tiles.shape[4]
    forward, backward = band_matrices(kernels, 2 * rows, Z_DEV, nx)
    backdrop = lax.dynamic_slice_in_dim(background, channel, 1, 0)

    table = table.reshape(2 * rows, 3)
    table = (table[:, 0].astype(jnp.int32), table[:, 1], table[:, 2])
    planes, over, (forward, backward, backdrop, table) = route_tiles(
        camera_tiles, tile_block, tile_offset, (forward, backward, backdrop, table)
    )
    blocks = lax.axis_size("bz")
    before = lax.ppermute(over.astype(jnp.float16), "bz", [(i, i + 1) for i in range(blocks - 1)])
    parts = deskew(backdrop, *table, planes)
    deskewed, *field = deskew_more(backdrop, *table, before.astype(F32), parts)

    half = lambda x, start: lax.dynamic_slice_in_dim(x, start, rows, 0)
    other_start = (1 - channel) * rows
    deskewed_other = swap_pair(half(deskewed, other_start))

    estimate = deskewed
    for iteration in range(ITERS):
        halos = halo_exchange(field)
        inner = blur_inner(True, field[0], forward[0])
        field = blur_outer(True, False, jnp.int32(0), backdrop, inner, halos, forward[1], deskewed)
        halos = halo_exchange(field)
        swap = channel * rows if iteration == ITERS - 1 else jnp.int32(0)
        inner = blur_inner(False, field[0], backward[0])
        estimate, peak, *field = blur_outer(False, iteration == 0, swap, backdrop, inner, halos, backward[1], estimate)
    theirs = estimate[rows:]
    power = jnp.floor(jnp.log2(jnp.max(peak))) - 13.0
    message = jnp.concatenate(
        [theirs * jnp.exp2(-power), jnp.full((1,) + theirs.shape[1:], power)], axis=0
    ).astype(jnp.float16)
    got = swap_pair(message)
    deskewed_out = place_other(channel, deskewed_other, place_own(channel, channel, deskewed))
    partial = place_own(channel, jnp.int32(0), estimate)
    received = got[:rows].astype(F32) * jnp.exp2(got[rows, 0, 0].astype(F32))
    return deskewed_out, place_other(channel, received, partial)


def solution(mesh):
    placed = (P("bz", None, "by", None, None), P(), P(), P("by"), P("by", None), P(), P())
    return jax.shard_map(
        shards,
        mesh=mesh,
        in_specs=placed,
        out_specs=(P(None, "by", "bz", None), P(None, "by", "bz", None)),
        check_vma=False,
    )
```

```python
import functools

import jax
import jax.numpy as jnp
from jax import lax
from jax.experimental import pallas as pl
from jax.experimental.pallas import tpu as pltpu
from jax.sharding import PartitionSpec as P


SHIFT = 8
ITERS = 2
Z_DEV = 64
HALO = 16
SPILL = 2
F32 = jnp.float32
BF16 = jnp.bfloat16


def in_vmem(count):
    return [pl.BlockSpec(memory_space=pltpu.VMEM) for _ in range(count)]


def place_own_kernel(channel_ref, part_ref, both_ref, out_ref, sem):
    rows = out_ref.shape[1]
    channel = channel_ref[0]
    copy = pltpu.make_async_copy(
        both_ref.at[pl.ds(pl.multiple_of(part_ref[0] * rows, 8), rows)], out_ref.at[channel], sem
    )
    copy.start()
    copy.wait()


def place_other_kernel(channel_ref, other_ref, partial_ref, out_ref, sem):
    copy = pltpu.make_async_copy(other_ref, out_ref.at[1 - channel_ref[0]], sem)
    copy.start()
    copy.wait()


def place_own(channel, part, both_rows, rows):
    return pl.pallas_call(
        place_own_kernel,
        out_shape=jax.ShapeDtypeStruct((2, rows) + both_rows.shape[1:], both_rows.dtype),
        in_specs=[pl.BlockSpec(memory_space=pltpu.SMEM)] * 2 + in_vmem(1),
        out_specs=pl.BlockSpec(memory_space=pl.ANY),
        scratch_shapes=[pltpu.SemaphoreType.DMA(())],
        compiler_params=pltpu.CompilerParams(vmem_limit_bytes=8 << 20),
        name="place_own",
    )(channel[None], part[None], both_rows)


def place_other(channel, other, partial):
    return pl.pallas_call(
        place_other_kernel,
        out_shape=jax.ShapeDtypeStruct(partial.shape, partial.dtype),
        in_specs=[pl.BlockSpec(memory_space=pltpu.SMEM)] + in_vmem(1) + [pl.BlockSpec(memory_space=pl.ANY)],
        out_specs=pl.BlockSpec(memory_space=pl.ANY),
        scratch_shapes=[pltpu.SemaphoreType.DMA(())],
        input_output_aliases={2: 0},
        compiler_params=pltpu.CompilerParams(vmem_limit_bytes=8 << 20),
        name="place_other",
    )(channel[None], other, partial)


def pack_kernel(own_ref, channel_ref, turn_ref, block_ref, tiles_ref, *rest, base, count):
    *based, keep_ref, flip_ref, seen_ref = rest
    channels, spill = tiles_ref.shape[1], keep_ref.shape[0]
    blocks = seen_ref.shape[0]
    for block in range(blocks):
        seen_ref[block] = 0

    def place(t, spilled):
        block = block_ref[own_ref[0] * count + t]
        slot = seen_ref[block]
        seen_ref[block] = slot + 1

        if based:

            @pl.when(slot < base)
            def _():
                for c in range(channels):
                    row = (c * blocks + block) * base + slot
                    based[0][row] = jnp.swapaxes(tiles_ref[t, c], 0, 1)

        late = slot >= base

        @pl.when(late & (spilled // spill == turn_ref[0]))
        def _():
            keep_ref[spilled % spill] = jnp.swapaxes(tiles_ref[t, channel_ref[0]], 0, 1)
            flip_ref[spilled % spill] = jnp.swapaxes(tiles_ref[t, 1 - channel_ref[0]], 0, 1)

        return spilled + late.astype(jnp.int32)

    lax.fori_loop(0, count, place, 0)


def pack_tiles(camera_tiles, tile_block, turn, base, with_base):
    count, channels, rows, planes, nx = camera_tiles.shape
    blocks = lax.axis_size("bz")
    shape = lambda *lead: jax.ShapeDtypeStruct(lead + (planes, rows, nx), camera_tiles.dtype)
    outs = [shape(SPILL), shape(SPILL)]
    if with_base:
        outs = [shape(channels * blocks * base)] + outs
    return pl.pallas_call(
        functools.partial(pack_kernel, base=base, count=count),
        out_shape=outs,
        in_specs=[pl.BlockSpec(memory_space=pltpu.SMEM)] * 4 + in_vmem(1),
        out_specs=in_vmem(len(outs)),
        scratch_shapes=[pltpu.SMEM((blocks,), jnp.int32)],
        compiler_params=pltpu.CompilerParams(vmem_limit_bytes=12 << 20),
        name="pack_tiles" if with_base else "pack_spill",
    )(lax.axis_index("bz")[None], (lax.axis_index("by") % 2)[None], turn[None], tile_block, camera_tiles)


def add_tile(planes_ref, here, start, tile):
    for s in range(tile.shape[0]):
        planes_ref[start + s, here, :] += tile[s].astype(F32)


def add_spill(planes_ref, channel_ref, starts_ref, spill_refs):
    for side, spill_ref in enumerate(spill_refs):
        sources, flips, spill, _, rows = spill_ref.shape[:5]
        for m in range(sources):
            for k in range(spill):
                start = starts_ref[(side * sources + m) * spill + k]

                @pl.when(start >= 0)
                def _():
                    for flip in range(flips):
                        half = channel_ref[0] if flip == 0 else 1 - channel_ref[0]
                        here = pl.ds(pl.multiple_of(half * rows, 8), rows)
                        add_tile(planes_ref, here, start, spill_ref[m, flip, k])


def gather_planes_kernel(channel_ref, starts_ref, spill_starts_ref, arrived_ref, one_ref, two_ref, planes_ref, tail_ref):
    halves, slots, _, rows = arrived_ref.shape[:4]
    height = planes_ref.shape[0]

    def clear(z, carry):
        planes_ref[z] = jnp.zeros(planes_ref.shape[1:], F32)
        return carry

    lax.fori_loop(0, height, clear, 0)

    def add(j, carry):
        start = starts_ref[j]

        @pl.when(start >= 0)
        def _():
            for h in range(halves):
                add_tile(planes_ref, pl.ds(h * rows, rows), start, arrived_ref[h, j])

        return carry

    lax.fori_loop(0, slots, add, 0)
    add_spill(planes_ref, channel_ref, spill_starts_ref, (one_ref, two_ref))
    tail_ref[...] = planes_ref[height - tail_ref.shape[0]:]


def gather_planes(channel, starts, spill_starts, arrived, spills):
    halves, _, planes, rows, nx = arrived.shape
    return pl.pallas_call(
        gather_planes_kernel,
        out_shape=[
            jax.ShapeDtypeStruct((Z_DEV + planes - 1, halves * rows, nx), F32),
            jax.ShapeDtypeStruct((SHIFT + planes, halves * rows, nx), F32),
        ],
        in_specs=[pl.BlockSpec(memory_space=pltpu.SMEM)] * 3 + in_vmem(3),
        out_specs=in_vmem(2),
        compiler_params=pltpu.CompilerParams(vmem_limit_bytes=16 << 20),
        name="gather_planes",
    )(channel[None], starts, spill_starts, arrived, *spills)


def more_planes_kernel(channel_ref, spill_starts_ref, one_ref, two_ref, planes_in_ref, planes_ref, tail_ref):
    planes_ref[...] = planes_in_ref[...]
    add_spill(planes_ref, channel_ref, spill_starts_ref, (one_ref, two_ref))
    tail_ref[...] = planes_ref[planes_ref.shape[0] - tail_ref.shape[0]:]


def more_planes(channel, spill_starts, spills, planes, tail):
    return pl.pallas_call(
        more_planes_kernel,
        out_shape=[jax.ShapeDtypeStruct(x.shape, x.dtype) for x in (planes, tail)],
        in_specs=[pl.BlockSpec(memory_space=pltpu.SMEM)] * 2 + in_vmem(3),
        out_specs=in_vmem(2),
        compiler_params=pltpu.CompilerParams(vmem_limit_bytes=24 << 20),
        name="more_planes",
    )(channel[None], spill_starts, *spills, planes)


def deskew_kernel(odd_ref, backdrop_ref, band_ref, near_ref, far_ref, planes_ref,
                  out_ref, cast_ref, out_a_ref, out_b_ref, all_ref, *, pitch):
    ny, nz = out_ref.shape[:2]
    ahead = SHIFT + 1
    backdrop = backdrop_ref[0]
    odd = odd_ref[0] == 1
    for z in range(ahead):
        all_ref[pl.ds(z * pitch, ny), :] = jnp.zeros((ny, all_ref.shape[1]), F32)
    for z in range(nz):
        all_ref[pl.ds((z + ahead) * pitch, ny), :] = planes_ref[z]

    def row(y, carry):
        first = (ahead - band_ref[y]) * pitch + y
        value = near_ref[y] * all_ref[pl.ds(first, nz, stride=pitch), :]
        value = value + far_ref[y] * all_ref[pl.ds(first - pitch, nz, stride=pitch), :]
        out_ref[y] = value
        cast = (value + backdrop).astype(BF16)
        cast_ref[y] = cast
        bottom, top = cast[:HALO], cast[nz - HALO:]
        out_a_ref[y] = jnp.where(odd, bottom, top)
        out_b_ref[y] = jnp.where(odd, top, bottom)
        return carry

    lax.fori_loop(0, ny, row, 0, unroll=4)


def deskew_more_kernel(odd_ref, backdrop_ref, band_ref, near_ref, far_ref, before_ref,
                       value_ref, cast_in_ref, a_ref, b_ref, out_ref, cast_ref, out_a_ref, out_b_ref, all_ref, *, pitch):
    ny = value_ref.shape[0]
    reach = before_ref.shape[0]
    ahead = SHIFT + 1
    backdrop = backdrop_ref[0]
    odd = odd_ref[0] == 1
    for z in range(ahead + HALO):
        plane = before_ref[z] if z < reach else jnp.zeros(before_ref.shape[1:], F32)
        all_ref[pl.ds(z * pitch, ny), :] = plane

    def row(y, carry):
        first = (ahead - band_ref[y]) * pitch + y
        value = near_ref[y] * all_ref[pl.ds(first, HALO, stride=pitch), :]
        value = value + far_ref[y] * all_ref[pl.ds(first - pitch, HALO, stride=pitch), :]
        value = value + value_ref[y, :HALO]
        out_ref[y, :HALO] = value
        cast = (value + backdrop).astype(BF16)
        cast_ref[y, :HALO] = cast
        out_a_ref[y] = jnp.where(odd, cast, a_ref[y])
        out_b_ref[y] = jnp.where(odd, b_ref[y], cast)
        return carry

    lax.fori_loop(0, ny, row, 0, unroll=8)


def deskew(backdrop, band, near, far, planes):
    ny, nx = planes.shape[1:]
    pitch = ny + 8
    smem = [pl.BlockSpec(memory_space=pltpu.SMEM)] * 5
    return pl.pallas_call(
        functools.partial(deskew_kernel, pitch=pitch),
        out_shape=[
            jax.ShapeDtypeStruct((ny, Z_DEV, nx), F32),
            jax.ShapeDtypeStruct((ny, Z_DEV, nx), BF16),
            jax.ShapeDtypeStruct((ny, HALO, nx), BF16),
            jax.ShapeDtypeStruct((ny, HALO, nx), BF16),
        ],
        in_specs=smem + in_vmem(1),
        out_specs=in_vmem(4),
        scratch_shapes=[pltpu.VMEM(((Z_DEV + SHIFT + 1) * pitch, nx), F32)],
        compiler_params=pltpu.CompilerParams(vmem_limit_bytes=24 << 20),
        cost_estimate=pl.CostEstimate(flops=5_000_000_000, transcendentals=0, bytes_accessed=12_000_000),
        name="deskew",
    )(odd_block(), backdrop, band, near, far, planes)


def deskew_more(backdrop, band, near, far, before, parts):
    ny, nx = before.shape[1:]
    pitch = ny + 8
    smem = [pl.BlockSpec(memory_space=pltpu.SMEM)] * 5
    return pl.pallas_call(
        functools.partial(deskew_more_kernel, pitch=pitch),
        out_shape=[jax.ShapeDtypeStruct(part.shape, part.dtype) for part in parts],
        in_specs=smem + in_vmem(5),
        out_specs=in_vmem(4),
        scratch_shapes=[pltpu.VMEM(((HALO + SHIFT + 1) * pitch, nx), F32)],
        input_output_aliases={6 + i: i for i in range(4)},
        compiler_params=pltpu.CompilerParams(vmem_limit_bytes=16 << 20),
        name="deskew_more",
    )(odd_block(), backdrop, band, near, far, before, *parts)


def pair_lanes(x, index, height):
    return jnp.concatenate(
        [x[index * height:(index + 1) * height], x[(index + 1) * height:(index + 2) * height]], axis=1
    )


def blur_x(pieces, mx):
    stack = jnp.concatenate(pieces, axis=0)
    return jnp.dot(jnp.concatenate([stack, stack], axis=1), mx, preferred_element_type=F32).astype(BF16)


def terms_of(column, coarse):
    head = column.astype(BF16)
    if coarse:
        return jnp.concatenate([head, head], axis=0)
    tail = (column - head.astype(F32)).astype(BF16)
    return jnp.concatenate([head, tail, head], axis=0)


def inner_kernel(own_ref, mx_ref, mz_ref, my_ref, out_ref, mid_ref, *, coarse):
    ny, nz, lanes = own_ref.shape
    pitch = nz + 8
    group = ny // 2
    ahead = 16

    def planes(g, carry):
        mz = mz_ref[...]
        alongx = blur_x([own_ref[g * group + k] for k in range(group)], mx_ref[...])
        for k in range(0, group, 4):
            first, second = pair_lanes(alongx, k, nz), pair_lanes(alongx, k + 2, nz)
            both = jnp.dot(
                mz, jnp.concatenate([first, first, second, second], axis=0), preferred_element_type=F32
            )
            row = pl.multiple_of((g * group + k) * pitch, 8)
            mid_ref[pl.ds(row, nz), :] = both[:nz, :lanes]
            mid_ref[pl.ds(row + pitch, nz), :] = both[:nz, lanes:]
            mid_ref[pl.ds(row + 2 * pitch, nz), :] = both[nz:, :lanes]
            mid_ref[pl.ds(row + 3 * pitch, nz), :] = both[nz:, lanes:]
        return carry

    lax.fori_loop(0, ny // group, planes, 0)

    def columns(g, carry):
        my = my_ref[:, ny:] if coarse else my_ref[...]
        for k in range(ahead):
            z = (g * ahead + k) * 2
            terms = [terms_of(mid_ref[pl.ds(z + i, ny, stride=pitch), :], coarse) for i in range(2)]
            both = jnp.dot(my, jnp.concatenate(terms, axis=1), preferred_element_type=F32)
            out_ref[pl.ds(z, ny, stride=pitch), :] = both[:, :lanes]
            out_ref[pl.ds(z + 1, ny, stride=pitch), :] = both[:, lanes:]
        return carry

    lax.fori_loop(0, nz // (2 * ahead), columns, 0)


def outer_kernel(odd_ref, swap_ref, backdrop_ref, inner_ref, a_ref, b_ref, side_ref, side_a_ref, side_b_ref,
                 mx_ref, mze_ref, mzs_ref, mye_ref, mys_ref, point_ref, *rest, quotient, first, last, ny, nz):
    if quotient:
        cast_ref, out_a_ref, out_b_ref, edge_ref, rim_ref, more_ref = rest
    elif last:
        mine_ref, theirs_ref, peak_ref, edge_ref, rim_ref, more_ref = rest
    else:
        full_ref, peak_ref, cast_ref, out_a_ref, out_b_ref, edge_ref, rim_ref, more_ref = rest
    nside = side_ref.shape[0]
    lanes = mx_ref.shape[1]
    pitch = nz + 8
    faces = 2 * HALO
    edge_pitch = faces + 8
    width = nz + faces
    many = ny // 2

    def face_planes(g, carry):
        pieces = []
        for k in range(many):
            pieces += [a_ref[g * many + k], b_ref[g * many + k]]
        mze = mze_ref[...]
        alongx = blur_x(pieces, mx_ref[...])
        for k in range(0, many, 8):
            pairs = []
            for p in range(4):
                pairs += [pair_lanes(alongx, k + 2 * p, faces)] * 2
            both = jnp.dot(mze, jnp.concatenate(pairs, axis=0), preferred_element_type=F32)
            for p in range(4):
                row = pl.multiple_of((g * many + k + 2 * p) * edge_pitch, 8)
                edge_ref[pl.ds(row, faces), :] = both[p * faces:(p + 1) * faces, :lanes]
                edge_ref[pl.ds(row + edge_pitch, faces), :] = both[p * faces:(p + 1) * faces, lanes:]
        return carry

    lax.fori_loop(0, ny // many, face_planes, 0)
    group = 16

    for g in range(nside // group):
        pieces = []
        for k in range(group):
            y = g * group + k
            pieces += [side_a_ref[y], side_ref[y], side_b_ref[y]]
        alongx = blur_x(pieces, mx_ref[...])
        for k in range(0, group, 2):
            pair = pair_lanes(alongx, k, width)
            both = jnp.dot(mzs_ref[...], jnp.concatenate([pair, pair], axis=0), preferred_element_type=F32)
            row = (g * group + k) * pitch
            rim_ref[pl.ds(row, nz), :] = both[:, :lanes]
            rim_ref[pl.ds(row + pitch, nz), :] = both[:, lanes:]

    def rim(z):
        return rim_ref[pl.ds(z, nside, stride=pitch), :]

    for z in range(0, nz, 2):
        if z < HALO or z >= nz - HALO:
            e = z if z < HALO else z - nz + faces
            terms = [
                terms_of(
                    jnp.concatenate([edge_ref[pl.ds(e + i, ny, stride=edge_pitch), :], rim(z + i)], axis=0), quotient
                )
                for i in range(2)
            ]
            mye = mye_ref[:, ny + nside:] if quotient else mye_ref[...]
            both = jnp.dot(mye, jnp.concatenate(terms, axis=1), preferred_element_type=F32)
        else:
            terms = [terms_of(rim(z + i), quotient) for i in range(2)]
            mys = mys_ref[:, nside:] if quotient else mys_ref[...]
            both = jnp.dot(mys, jnp.concatenate(terms, axis=1), preferred_element_type=F32)
        more_ref[pl.ds(z, ny, stride=pitch), :] = both[:, :lanes]
        more_ref[pl.ds(z + 1, ny, stride=pitch), :] = both[:, lanes:]

    backdrop = backdrop_ref[0]
    odd = odd_ref[0] == 1
    swap = swap_ref[0]

    def finish(y, carry):
        row = pl.multiple_of(y * pitch, 8)
        blurred = inner_ref[pl.ds(row, nz), :] + more_ref[pl.ds(row, nz), :]
        if quotient:
            value = point_ref[y] / (blurred + backdrop)
        else:
            value = (point_ref[y] + backdrop if first else point_ref[y]) * blurred
            full_ref[y ^ swap] = value
            carry = jnp.maximum(carry, value)
        cast = value.astype(BF16)
        cast_ref[y] = cast
        bottom, top = cast[:HALO], cast[nz - HALO:]
        out_a_ref[y] = jnp.where(odd, bottom, top)
        out_b_ref[y] = jnp.where(odd, top, bottom)
        return carry

    if last:
        half = ny // 2

        def finish_half(ref, start):
            def step(i, carry):
                y = i + start
                row = pl.multiple_of(y * pitch, 8)
                blurred = inner_ref[pl.ds(row, nz), :] + more_ref[pl.ds(row, nz), :]
                value = (point_ref[y] + backdrop if first else point_ref[y]) * blurred
                ref[i] = value
                return jnp.maximum(carry, value)

            return lax.fori_loop(0, half, step, jnp.zeros((nz, lanes), F32), unroll=8)

        peak_ref[...] = finish_half(theirs_ref, half - swap)
        finish_half(mine_ref, swap)
        return

    peak = lax.fori_loop(0, ny, finish, 0 if quotient else jnp.zeros((nz, lanes), F32), unroll=8)
    if not quotient:
        peak_ref[...] = peak


def blur_inner(coarse, block, matrices):
    ny, nz, nx = block.shape
    return pl.pallas_call(
        functools.partial(inner_kernel, coarse=coarse),
        out_shape=jax.ShapeDtypeStruct((ny * (nz + 8), nx), F32),
        in_specs=in_vmem(4),
        out_specs=in_vmem(1)[0],
        scratch_shapes=[pltpu.VMEM((ny * (nz + 8), nx), F32)],
        compiler_params=pltpu.CompilerParams(vmem_limit_bytes=20 << 20),
        cost_estimate=pl.CostEstimate(flops=20_000_000_000, transcendentals=0, bytes_accessed=8_000_000),
        name="blur_inner",
    )(block, *matrices)


def blur_outer(quotient, first, last, swap, backdrop, inner, halos, matrices, point):
    ny, nz, nx = point.shape
    nside = halos[2].shape[0]
    outs = [
        jax.ShapeDtypeStruct((ny, nz, nx), BF16),
        jax.ShapeDtypeStruct((ny, HALO, nx), BF16),
        jax.ShapeDtypeStruct((ny, HALO, nx), BF16),
    ]
    if last:
        part = jax.ShapeDtypeStruct((ny // 2, nz, nx), F32)
        outs = [part, part, jax.ShapeDtypeStruct((nz, nx), F32)]
    elif not quotient:
        outs = [jax.ShapeDtypeStruct((ny, nz, nx), F32), jax.ShapeDtypeStruct((nz, nx), F32)] + outs
    return pl.pallas_call(
        functools.partial(outer_kernel, quotient=quotient, first=first, last=last, ny=ny, nz=nz),
        out_shape=outs,
        in_specs=[pl.BlockSpec(memory_space=pltpu.SMEM)] * 3 + in_vmem(12),
        out_specs=in_vmem(len(outs)),
        scratch_shapes=[
            pltpu.VMEM((ny * (2 * HALO + 8), nx), F32),
            pltpu.VMEM((nside * (nz + 8), nx), F32),
            pltpu.VMEM((ny * (nz + 8), nx), F32),
        ],
        compiler_params=pltpu.CompilerParams(vmem_limit_bytes=32 << 20),
        cost_estimate=pl.CostEstimate(flops=10_000_000_000, transcendentals=0, bytes_accessed=16_000_000),
        name="blur_quotient" if quotient else "blur_estimate",
    )(odd_block(), swap[None], backdrop, inner, *halos, *matrices, point)


def odd_block():
    return (lax.axis_index("bz") % 2)[None]


def partners(count):
    phases = [[(i, i ^ 1) for i in range(count)]]
    if count > 2:
        phases.append([(i, ((i + 1) ^ 1) - 1) for i in range(1, count - 1)])
    return phases


def halo_exchange(field):
    block, *faces = field
    rows = block.shape[0]
    blocks = lax.axis_size("bz")
    odd = (lax.axis_index("by") // 2) % 2
    z_phases = partners(blocks)
    ends = [jnp.where(odd == 1, 0, rows - HALO), jnp.where(odd == 1, rows - HALO, 0)]
    sides = []
    corners = [[] for _ in z_phases]
    across = []
    for face, z_pairs in zip(faces, z_phases):
        across.append(lax.ppermute(face, "bz", z_pairs))
    for start, pairs in zip(ends, partners(lax.axis_size("by") // 2)):
        pairs = [(2 * a + c, 2 * b + c) for a, b in pairs for c in range(2)]
        sides.append(lax.ppermute(lax.dynamic_slice_in_dim(block, start, HALO, 0), "by", pairs))
        for face, z_pairs, found in zip(faces, z_phases, corners):
            both = [(a * blocks + p, b * blocks + q) for a, b in pairs for p, q in z_pairs]
            found.append(lax.ppermute(lax.dynamic_slice_in_dim(face, start, HALO, 0), ("by", "bz"), both))
    join = lambda parts: parts[0] if len(parts) == 1 else jnp.concatenate(parts, axis=0)
    return *across, join(sides), *[join(found) for found in corners]


def cut(index, size, count):
    block = jnp.zeros(index.shape, jnp.int32)
    for k in range(1, count):
        block = block + (index >= k * size).astype(jnp.int32)
    return block, index - block * size


def matrix_kernel(place_ref, taps_ref, *refs, nx, ny, nz, sides):
    count = taps_ref.shape[0] // 3
    odd_y, odd_z = place_ref[0] == 1, place_ref[1] == 1
    face_a = jnp.where(odd_z, -HALO, nz)
    face_b = jnp.where(odd_z, nz, -HALO)
    side_places = [jnp.where(odd_y, -HALO, ny), jnp.where(odd_y, ny, -HALO)][:sides]

    def fill(ref, axis, reverse, places):
        row = lax.broadcasted_iota(jnp.int32, ref.shape, 0)
        lane = lax.broadcasted_iota(jnp.int32, ref.shape, 1)
        offset, tail, kept = places(row, lane)
        offset = offset + count // 2
        matrix = jnp.zeros(ref.shape, F32)
        for t in range(count):
            tap = taps_ref[axis * count + (count - 1 - t if reverse else t)]
            matrix = jnp.where(offset == t, tap, matrix)
        if kept is not None:
            matrix = jnp.where(kept, matrix, 0.0)
        head = matrix.astype(BF16).astype(F32)
        ref[...] = jnp.where(tail, matrix - head, head).astype(BF16)

    def along_x(row, lane):
        part, source = cut(row, nx, 2)
        return source - lane, part == 1, None

    def along_z(row, lane):
        block, out = cut(row, nz, 2)
        lane_block, rest = cut(lane, 2 * nz, 2)
        part, source = cut(rest, nz, 2)
        return source - out, part == 1, block == lane_block

    def face_place(face):
        return jnp.where(face < HALO, face + face_a, face - HALO + face_b)

    def along_edges(row, lane):
        faces = 2 * HALO
        block, edge = cut(row, faces, 4)
        lane_block, rest = cut(lane, 2 * faces, 4)
        part, face = cut(rest, faces, 2)
        out = jnp.where(edge < HALO, edge, edge - faces + nz)
        return face_place(face) - out, part == 1, block == lane_block

    def along_rim(row, lane):
        part, column = cut(lane, nz + 2 * HALO, 2)
        source = jnp.where(
            column < HALO,
            column + face_a,
            jnp.where(column < HALO + nz, column - HALO, column - HALO - nz + face_b),
        )
        return source - row, part == 1, None

    def side_place(column):
        place = column + side_places[0]
        for k in range(1, sides):
            place = jnp.where(column >= k * HALO, column - k * HALO + side_places[k], place)
        return place

    def along_y(row, lane):
        part, column = cut(lane, ny, 3)
        return column - row, part == 2, None

    def along_y_edges(row, lane):
        part, column = cut(lane, ny + sides * HALO, 3)
        source = jnp.where(column < ny, column, side_place(column - ny))
        return source - row, part == 2, None

    def along_y_sides(row, lane):
        part, column = cut(lane, sides * HALO, 3)
        return side_place(column) - row, part == 2, None

    plan = ((2, along_x), (1, along_z), (0, along_y), (1, along_edges), (1, along_rim),
            (0, along_y_edges), (0, along_y_sides))
    for index, (axis, places) in enumerate(plan):
        for turn in range(2):
            fill(refs[turn * len(plan) + index], axis, turn == 1, places)


def band_matrices(kernels, ny, nz, nx):
    place = jnp.stack([(lax.axis_index("by") // 2) % 2, lax.axis_index("bz") % 2])
    sides = len(partners(lax.axis_size("by") // 2))
    shapes = [
        (2 * nx, nx),
        (2 * nz, 4 * nz),
        (ny, 3 * ny),
        (8 * HALO, 16 * HALO),
        (nz, 2 * (nz + 2 * HALO)),
        (ny, 3 * (ny + sides * HALO)),
        (ny, 3 * sides * HALO),
    ]
    found = pl.pallas_call(
        functools.partial(matrix_kernel, nx=nx, ny=ny, nz=nz, sides=sides),
        out_shape=[jax.ShapeDtypeStruct(shape, BF16) for shape in shapes * 2],
        in_specs=[pl.BlockSpec(memory_space=pltpu.SMEM)] * 2,
        out_specs=in_vmem(2 * len(shapes)),
        compiler_params=pltpu.CompilerParams(vmem_limit_bytes=8 << 20),
        name="band_matrices",
    )(place, kernels.reshape(-1))
    turns = [found[: len(shapes)], found[len(shapes):]]
    return [((mx, mz, my), (mx, mze, mzs, mye, mys)) for mx, mz, my, mze, mzs, mye, mys in turns]


def swap_pair(x):
    return lax.ppermute(x, "by", [(i, i ^ 1) for i in range(lax.axis_size("by"))])


def stack_kernel(*refs):
    *parts, out_ref = refs
    for i, part in enumerate(parts):
        out_ref[i] = part[...]


def stack_parts(parts):
    return pl.pallas_call(
        stack_kernel,
        out_shape=jax.ShapeDtypeStruct((len(parts),) + parts[0].shape, parts[0].dtype),
        in_specs=in_vmem(len(parts)),
        out_specs=in_vmem(1)[0],
        compiler_params=pltpu.CompilerParams(vmem_limit_bytes=12 << 20),
        name="stack_parts",
    )(*parts)


def share_spill(spill):
    blocks = lax.axis_size("bz")
    wide = lax.axis_size("by")
    found = []
    for m in range(0, blocks, 2):
        for flip in range(2):
            piece = spill[flip]
            if m or flip:
                pairs = [(b * blocks + z, (b ^ flip) * blocks + (z ^ m)) for b in range(wide) for z in range(blocks)]
                piece = lax.ppermute(piece, ("by", "bz"), pairs)
            found.append(piece)
    line = stack_parts(found)
    line = line.reshape((blocks // 2, 2) + line.shape[1:])
    return line, lax.ppermute(line, "bz", [(z, z ^ 1) for z in range(blocks)])


def route_tiles(camera_tiles, tile_block, tile_offset, prepared):
    count = camera_tiles.shape[0]
    blocks = lax.axis_size("bz")
    wide = lax.axis_size("by")
    base = max(1, count // blocks)
    own = lax.axis_index("bz")
    channel = lax.axis_index("by") % 2
    named = tile_block[:, 0]
    outgoing, *spill = pack_tiles(camera_tiles, named, jnp.int32(0), base, True)
    groups = [
        [(2 * j + c) * blocks + z for c in range(2) for z in range(blocks)] for j in range(wide // 2)
    ]
    arrived = lax.all_to_all(
        outgoing.reshape((2 * blocks, base) + outgoing.shape[1:]),
        ("by", "bz"), split_axis=0, concat_axis=0, axis_index_groups=groups, tiled=True,
    )
    targets = named.reshape(blocks, count)
    offsets = tile_offset.reshape(blocks, count)
    same = (targets[:, :, None] == targets[:, None, :]) & jnp.tri(count, k=-1, dtype=bool)[None]
    places = jnp.sum(same.astype(jnp.int32), axis=2)
    late = places >= base
    order = jnp.sum(jnp.where(late[:, None, :] & jnp.tri(count, k=-1, dtype=bool)[None], 1, 0), axis=2)
    mine = targets == own
    pick = lambda chosen: jnp.sum(jnp.where(chosen, offsets[:, :, None] + 1, 0), axis=1) - 1
    starts = pick(mine[:, :, None] & (places[:, :, None] == jnp.arange(base))).reshape(-1)
    sources = jnp.concatenate([(own ^ core) ^ jnp.arange(0, blocks, 2) for core in range(2)])

    def spill_starts(turn):
        chosen = (mine & late)[:, :, None] & (order[:, :, None] == turn * SPILL + jnp.arange(SPILL))
        return jnp.take(pick(chosen), sources, axis=0, mode="clip").reshape(-1)

    turns = (jnp.max(jnp.sum(late.astype(jnp.int32), axis=1)) + SPILL - 1) // SPILL
    spills = share_spill(spill)
    arrived = arrived.reshape((2, blocks * base) + arrived.shape[2:])
    starts, prepared = lax.optimization_barrier((starts, prepared))
    planes, tail = gather_planes(channel, starts, spill_starts(0), arrived, spills)

    def turn_step(carry):
        turn, planes, tail = carry
        again = pack_tiles(camera_tiles, named, turn, base, False)
        planes, tail = more_planes(channel, spill_starts(turn), share_spill(again), planes, tail)
        return turn + 1, planes, tail

    planes, tail = lax.cond(
        turns > 1,
        lambda planes, tail: lax.while_loop(lambda c: c[0] < turns, turn_step, (jnp.int32(1), planes, tail))[1:],
        lambda planes, tail: (planes, tail),
        planes,
        tail,
    )
    return planes, tail, prepared


def pair_stack(first_is_own, own, other):
    return jnp.stack([jnp.where(first_is_own, own, other), jnp.where(first_is_own, other, own)])


def shards(camera_tiles, tile_block, tile_offset, band_index, interp, psf_taps, background):
    channel = lax.axis_index("by") % 2
    first = channel == 0
    rows = camera_tiles.shape[2]
    table = jnp.concatenate([band_index[:, None].astype(F32), interp.astype(F32)], axis=1)
    table = pair_stack(first, table, swap_pair(table))

    taps = lax.dynamic_index_in_dim(psf_taps, channel, 0, keepdims=False)
    kernels = taps / jnp.sum(taps, axis=1, keepdims=True)
    nx = camera_tiles.shape[4]
    forward, backward = band_matrices(kernels, 2 * rows, Z_DEV, nx)
    backdrop = lax.dynamic_slice_in_dim(background, channel, 1, 0)

    table = table.reshape(2 * rows, 3)
    table = (table[:, 0].astype(jnp.int32), table[:, 1], table[:, 2])
    planes, over, (forward, backward, backdrop, table) = route_tiles(
        camera_tiles, tile_block, tile_offset, (forward, backward, backdrop, table)
    )
    blocks = lax.axis_size("bz")
    before = lax.ppermute(over.astype(jnp.float16), "bz", [(i, i + 1) for i in range(blocks - 1)])
    parts = deskew(backdrop, *table, planes)
    deskewed, *field = deskew_more(backdrop, *table, before.astype(F32), parts)

    half = lambda x, start: lax.dynamic_slice_in_dim(x, start, rows, 0)
    other_start = (1 - channel) * rows
    deskewed_other = swap_pair(half(deskewed, other_start))

    estimate = deskewed
    for iteration in range(ITERS):
        halos = halo_exchange(field)
        inner = blur_inner(True, field[0], forward[0])
        field = blur_outer(True, False, False, jnp.int32(0), backdrop, inner, halos, forward[1], deskewed)
        halos = halo_exchange(field)
        swap = channel * rows if iteration == ITERS - 1 else jnp.int32(0)
        inner = blur_inner(False, field[0], backward[0])
        last = iteration == ITERS - 1
        estimate, peak, *field = blur_outer(
            False, iteration == 0, last, swap, backdrop, inner, halos, backward[1], estimate
        )
    mine, theirs, peak = estimate, peak, field[0]
    power = jnp.floor(jnp.log2(jnp.max(peak))) - 13.0
    message = jnp.concatenate(
        [theirs * jnp.exp2(-power), jnp.full((1,) + theirs.shape[1:], power)], axis=0
    ).astype(jnp.float16)
    got = swap_pair(message)
    deskewed_out = place_other(channel, deskewed_other, place_own(channel, channel, deskewed, rows))
    partial = place_own(channel, jnp.int32(0), mine, rows)
    received = got[:rows].astype(F32) * jnp.exp2(got[rows, 0, 0].astype(F32))
    return deskewed_out, place_other(channel, received, partial)


def solution(mesh):
    placed = (P("bz", None, "by", None, None), P(), P(), P("by"), P("by", None), P(), P())
    return jax.shard_map(
        shards,
        mesh=mesh,
        in_specs=placed,
        out_specs=(P(None, "by", "bz", None), P(None, "by", "bz", None)),
        check_vma=False,
    )
```
